256 devices in a mesh: prompt: 4 (over x), vocab: 64 (over z, y, core).
Axes of the slice: x: 4, y: 4, z: 8, core: 2. Of those that a mesh axis runs over, the one named last changes fastest.
Arguments:
- hidden: bfloat16 [512, 8192], P('prompt')
- head: bfloat16 [8192, 65536], P('prompt', 'vocab')
- gain: float32 [8192], replicated, may hold values from 0.25 to 1.75
- refusal_ids: int32 [512, 16], P('prompt'), may hold values from 0 to 65535, as said below
- refusal_count: int32 [512], P('prompt'), may hold values from 1 to 16
- loss_scale: float32 [512], P('prompt'), may hold values from 8 to 32
Outputs:
- grad_hidden: float32 [512, 8192], P('prompt', 'vocab')
- log_refusal: float32 [512], P('prompt')
The draws below stay inside these ranges and needn't reach their ends.
Inputs may be any that keep to these rules, and one draw needn't show every extreme that they name: `refusal_ids`: the first refusal_count entries of a prompt's list are distinct ids below 65536; later entries are ignored.
All inputs are finite; a program needn't handle non-finite values.
Results may differ from the reference program's by a relative error of at most 0.0027.
The reference program's roundings to bfloat16 on the way (of `normed` and `grad_logits`) count: a program that leaves them out, or rounds other values in their place, can miss the bound.
Values may be sent and summed in bfloat16 or wider, within the bound.
A program may use at most 128 MiB of HBM per device.

```python
import math
import jax
import jax.numpy as jnp
from jax import lax

D = 8192
VOCAB = 65536
K = 16
PROMPTS = 512


def special_parts(key):
    base = jax.random.fold_in(key, 5)
    rows_pick = jax.random.permutation(jax.random.fold_in(base, 1), PROMPTS)[:4]
    quarter = VOCAB // 4
    first_cols = jnp.arange(4) * quarter + jax.random.randint(jax.random.fold_in(base, 2), (4,), 0, quarter - 1)
    strength = jnp.array([1.5, 2.2, 3.0, 4.0], jnp.float32)
    leading = jax.random.normal(jax.random.fold_in(base, 3), (D, 4), jnp.float32) * strength * (60.0 / D)
    nearby = leading * (1.0 - 2.0 / (60.0 * strength)) + 0.3 / math.sqrt(D) * jax.random.normal(jax.random.fold_in(base, 4), (D, 4), jnp.float32)
    return (rows_pick, first_cols, strength, leading, nearby)


def draw_hidden(key, part):
    drawn = jax.random.normal(jax.random.fold_in(key, 11), (PROMPTS, D), jnp.float32)
    rows_pick, first_cols, strength, leading, nearby = special_parts(key)
    aligned = leading.T * (D / (60.0 * strength[:, None]))
    aligned = aligned + 0.05 * jax.random.normal(jax.random.fold_in(key, 14), (4, D), jnp.float32)
    drawn = drawn.at[rows_pick].set(aligned)
    return drawn.astype(jnp.bfloat16)


def draw_head(key, part):
    col_scale = jnp.exp(jax.random.uniform(jax.random.fold_in(key, 21), (1, VOCAB), jnp.float32, math.log(0.25), math.log(2.5)))
    shared = jax.random.normal(jax.random.fold_in(key, 23), (D, 1), jnp.float32)
    drawn = jax.random.normal(jax.random.fold_in(key, 22), (D, VOCAB), jnp.float32)
    drawn = (drawn + 0.6 * shared) * col_scale / math.sqrt(D)
    rows_pick, first_cols, strength, leading, nearby = special_parts(key)
    drawn = drawn.at[:, first_cols].set(leading)
    drawn = drawn.at[:, first_cols + 1].set(nearby)
    return drawn.astype(jnp.bfloat16)


def draw_refusal_ids(key, part):
    span_size = VOCAB // K
    offsets = jax.random.randint(jax.random.fold_in(key, 31), (PROMPTS, K), 0, span_size)
    offsets = offsets.at[0, K - 1].set(span_size - 1)
    offsets = offsets.at[1, 0].set(0)
    return (jnp.arange(K)[None, :] * span_size + offsets).astype(jnp.int32)


def draw_refusal_count(key, part):
    counts = jax.random.randint(jax.random.fold_in(key, 32), (PROMPTS,), 1, K + 1)
    position = jnp.arange(PROMPTS)
    counts = jnp.where(position % 7 == 0, K, counts)
    counts = jnp.where(position % 7 == 3, 1, counts)
    return counts.astype(jnp.int32)


def level_of(own_key, dims, split, low, top_value):
    level, own = 1.0, jax.random.fold_in(own_key, 6)
    for dim, parts in split:
        draws = jnp.exp(jax.random.uniform(jax.random.fold_in(own, dim), (parts,), jnp.float32, low / len(split), top_value / len(split)))
        level = level * jnp.repeat(draws, dims[dim] // parts).reshape([-1 if axis == dim else 1 for axis in range(len(dims))])
    return level


def setup_inputs(seed: int = 0) -> dict:
    streams_of = jax.random.split(jax.random.key(seed), 7)
    hidden = draw_hidden(jax.random.fold_in(streams_of[6], 71), 0)
    head = draw_head(jax.random.fold_in(streams_of[6], 71), 0)
    gain = jnp.clip(1.0 + 0.15 * jax.random.normal(streams_of[2], (D,), jnp.float32), 0.25, 1.75)
    refusal_ids = draw_refusal_ids(jax.random.fold_in(streams_of[6], 71), 0)
    refusal_count = draw_refusal_count(jax.random.fold_in(streams_of[6], 71), 0)
    loss_scale = jnp.clip(8.0 + 24.0 * jax.random.uniform(streams_of[5], (PROMPTS,), jnp.float32) ** level_of(streams_of[5], (PROMPTS,), ((0, 4),), -0.2, 0.2), 8.0, 32.0)
    return dict(hidden=hidden, head=head, gain=gain, refusal_ids=refusal_ids, refusal_count=refusal_count, loss_scale=loss_scale)


epsilon = 1e-05
lowest = -1e+30

def reference(hidden, head, gain, refusal_ids, refusal_count, loss_scale):
    hidden_f = hidden.astype(jnp.float32)
    inverse_rms = lax.rsqrt(lax.optimization_barrier(jnp.mean(hidden_f * hidden_f, axis=1, keepdims=True)) + epsilon)
    normed = (hidden_f * inverse_rms * gain).astype(jnp.bfloat16)
    logits = jnp.dot(normed, head, preferred_element_type=jnp.float32)
    in_list = jnp.arange(K)[None, :] < refusal_count[:, None]
    picked = jnp.take_along_axis(logits, refusal_ids, axis=1)
    peak_all = lax.optimization_barrier(jnp.max(logits, axis=1))
    peak_ref = lax.optimization_barrier(jnp.max(jnp.where(in_list, picked, lowest), axis=1))
    sum_all = lax.optimization_barrier(jnp.sum(jnp.exp(logits - peak_all[:, None]), axis=1))
    sum_ref = lax.optimization_barrier(jnp.sum(jnp.exp(jnp.where(in_list, picked - peak_ref[:, None], lowest)), axis=1))
    lse_all = peak_all + jnp.log(sum_all)
    lse_ref = peak_ref + jnp.log(sum_ref)
    log_refusal = lse_ref - lse_all
    row_index = jnp.arange(PROMPTS).astype(jnp.int32)[:, None]
    member = jnp.zeros(logits.shape, jnp.int32).at[row_index, refusal_ids].max(in_list.astype(jnp.int32)) > 0
    grad_logits = loss_scale[:, None] * (jnp.exp(jnp.where(member, logits - lse_ref[:, None], lowest)) - jnp.exp(logits - lse_all[:, None]))
    grad_b = grad_logits.astype(jnp.bfloat16)
    grad_normed = jnp.dot(grad_b, head.T, preferred_element_type=jnp.float32)
    row_term = lax.optimization_barrier(jnp.sum(grad_normed * normed.astype(jnp.float32), axis=1))
    grad_hidden = inverse_rms * gain * grad_normed - hidden_f * (inverse_rms * inverse_rms / D) * row_term[:, None]
    return (grad_hidden, log_refusal)
```

```python
import functools

import jax
import jax.numpy as jnp
from jax import lax
from jax.experimental import pallas as pl
from jax.experimental.pallas import tpu as pltpu
from jax.sharding import PartitionSpec as P

epsilon = 1e-05
lowest = -1e30
f32 = jnp.float32
bf16 = jnp.bfloat16

NX, NY, NZ, NC = 4, 4, 8, 2
R = 128
DL = 2048
VL = 1024
T = 256
KT = DL // T
VT = VL // T


class Wires:
    def __init__(self, send, recv):
        self.send, self.recv, self.used, self.open = send, recv, 0, []

    def describe(self, src, dst, device, index):
        return pltpu.make_async_remote_copy(
            src_ref=src,
            dst_ref=dst,
            send_sem=self.send.at[index],
            recv_sem=self.recv.at[index],
            device_id=device,
            device_id_type=pl.DeviceIdType.MESH,
        )

    def start(self, src, dst, device):
        copy = self.describe(src, dst, device, self.used)
        self.used += 1
        copy.start()
        self.open.append(copy)
        return copy

    def close(self):
        for copy in self.open:
            copy.wait_send()


def kernel(
    hid_hbm, head_hbm, gain_ref, ids_ref, count_ref, loss_ref, grad_ref, log_ref,
    hid, head, inv_v, nsend, nrm, ptwo, pright, pleft, pown, hl, hr, inl, inr,
    mask, eall, eref, st1, st2, rs1, rs2, gt, csend, crecv, own32,
    ytwo, yright, yleft, yhl, yhr, yinl, yinr, fsend, frecv,
    load_sems, send_sems, recv_sems, fsend_sems, frecv_sems,
):
    p = lax.axis_index("prompt")
    v = lax.axis_index("vocab")
    c = v % NC
    y = (v // NC) % NY
    z = v // (NC * NY)

    def at(x_=p, y_=y, z_=z, c_=c):
        return (x_, (z_ * NY + y_) * NC + c_)

    def x_by(d):
        return at(x_=(p + d) % NX)

    def y_by(d):
        return at(y_=(y + d) % NY)

    def z_by(d):
        return at(z_=(z + d) % NZ)

    j_own = y * NC + c

    def plane_by(d):
        j = (j_own + d) % (NY * NC)
        return at(y_=j // NC, c_=j % NC), j

    sibling = at(c_=1 - c)

    load_hid = pltpu.make_async_copy(hid_hbm, hid, load_sems.at[0])
    load_head = pltpu.make_async_copy(head_hbm, head, load_sems.at[1])
    load_hid.start()
    load_head.start()

    barrier = pltpu.get_barrier_semaphore()

    def greet(device):
        pl.semaphore_signal(
            barrier, inc=1, device_id=device, device_id_type=pl.DeviceIdType.MESH
        )

    for d in range(1, NX):
        greet(x_by(d))
    for d in range(1, NY * NC):
        greet(plane_by(d)[0])
    for d in range(1, NZ):
        greet(z_by(d))
    source = z // 2
    foreign = source != p
    for d in range(1, NX):
        for zl in range(2):

            @pl.when(z != 2 * p + zl)
            def _():
                greet(at(x_=(p + d) % NX, z_=2 * p + zl))

    for zs in range(NZ):

        @pl.when(jnp.logical_and(foreign, jnp.logical_and(zs != z, zs // 2 != p)))
        def _():
            greet(at(x_=source, z_=zs))

    wires = Wires(send_sems, recv_sems)

    lane = lax.broadcasted_iota(jnp.int32, (R, 128), 1)
    sub = lax.broadcasted_iota(jnp.int32, (R, 128), 0)

    def columns_of(rows):
        return jnp.concatenate([rows, jnp.zeros((R - 8, 128), f32)], axis=0).T

    load_hid.wait()

    def square(j, acc):
        x = hid[:, pl.ds(pl.multiple_of(j * 1024, 1024), 1024)].astype(f32)
        x = x * x
        for i in range(8):
            acc = acc + x[:, i * 128 : (i + 1) * 128]
        return acc

    acc = lax.fori_loop(0, 8, square, jnp.zeros((R, 128), f32))
    inv = lax.rsqrt(jnp.sum(acc, axis=1, keepdims=True) / 8192.0 + epsilon)
    inv_v[...] = jnp.broadcast_to(inv, (R, 128))

    def normed(col):
        col = pl.multiple_of(col, T)
        x = hid[:, pl.ds(col, T)].astype(f32)
        return (x * inv * gain_ref[:, pl.ds(col, T)]).astype(bf16)

    for d in (2, 1, 3):
        q = (p + d) % NX
        for j in range(4):
            nsend[d - 1, j] = normed(q * DL + (c * 4 + j) * T)

    met = (NX - 1) + (NY * NC - 1) + (NZ - 1)
    pl.semaphore_wait(barrier, met + jnp.where(foreign, 2 * NX + 3, NX - 1))

    half = pl.ds(c * 4, 4)
    ncopy = {}
    for d in (2, 1, 3):
        slot = NX - d
        ncopy[slot] = wires.start(nsend.at[d - 1], nrm.at[slot, half], x_by(d))
    for k in range(KT):
        nrm[0, k] = normed(p * DL + k * T)
    share = {}
    for slot in (2, 3, 1):
        ncopy[slot].wait_recv()
        share[slot] = wires.start(nrm.at[slot, half], nrm.at[slot, half], sibling)
    other = pl.ds((1 - c) * 4, 4)
    share_sems = {slot: i for i, slot in enumerate((2, 3, 1), wires.used - 3)}

    def wait_share(slot):
        wires.describe(
            nrm.at[slot, other], nrm.at[slot, other], sibling, share_sems[slot]
        ).wait_recv()

    load_head.wait()

    def partial(s, t):
        lhs = jnp.concatenate([nrm[s, k] for k in range(KT)], axis=1)
        return jnp.dot(lhs, head[:, t * T : (t + 1) * T], preferred_element_type=f32)

    right, left = x_by(1), x_by(NX - 1)
    wait_share(2)
    ch_l, ch_r, cin_l, cin_r = {}, {}, {}, {}
    for t in (0, 2, 1, 3):
        ptwo[t] = partial(2, t)
        if t < 2:
            ch_l[t] = wires.start(ptwo.at[t], hl.at[t], right)
        else:
            ch_r[t - 2] = wires.start(ptwo.at[t], hr.at[t - 2], left)
    wait_share(1)
    for t in (2, 3):
        pright[t] = partial(1, t)
        cin_l[t] = wires.start(pright.at[t], inl.at[t], right)
    wait_share(3)
    for t in (0, 1):
        pleft[t] = partial(3, t)
        cin_r[t] = wires.start(pleft.at[t], inr.at[t], left)
    for t in (0, 1):
        pright[t] = partial(1, t)
        pleft[t + 2] = partial(3, t + 2)
    for t in (0, 1):
        ch_l[t].wait_recv()
        pright[t] = pright[t] + hl[t]
        cin_l[t] = wires.start(pright.at[t], inl.at[t], right)
        ch_r[t].wait_recv()
        pleft[t + 2] = pleft[t + 2] + hr[t]
        cin_r[t + 2] = wires.start(pleft.at[t + 2], inr.at[t + 2], left)
    for t in range(VT):
        pown[t] = partial(0, t)

    cl = jnp.where(
        sub == 0,
        jnp.broadcast_to(count_ref[...].astype(f32), (R, 128)),
        jnp.where(sub == 1, jnp.broadcast_to(loss_ref[...], (R, 128)), 0.0),
    ).T
    count_col, loss_col = cl[:, 0:1], cl[:, 1:2]
    wide = lax.broadcasted_iota(jnp.int32, (R, T), 1)
    for t in range(VT):
        hit = jnp.zeros((R, T), jnp.int32)
        for k in range(16):
            here = ids_ref[:, k : k + 1] - (v * VL + t * T)
            here = jnp.where(count_col > float(k), here, -1)
            hit = jnp.where(wide == here, 1, hit)
        mask[t] = hit

    m_all = jnp.full((R, T), -3e38, f32)
    m_ref = jnp.full((R, T), lowest, f32)
    for t in (2, 3, 0, 1):
        cin_l[t].wait_recv()
        cin_r[t].wait_recv()
        logit = pown[t] + inl[t] + inr[t]
        pown[t] = logit
        m_all = jnp.maximum(m_all, logit)
        m_ref = jnp.maximum(m_ref, jnp.where(mask[t] > 0, logit, lowest))
    m_all = jnp.max(m_all, axis=1, keepdims=True)
    m_ref = jnp.max(m_ref, axis=1, keepdims=True)
    s_all = jnp.zeros((R, T), f32)
    s_ref = jnp.zeros((R, T), f32)
    for t in range(VT):
        logit = pown[t]
        e = jnp.exp(logit - m_all)
        r = jnp.exp(jnp.where(mask[t] > 0, logit - m_ref, lowest))
        eall[t] = e
        eref[t] = r
        s_all = s_all + e
        s_ref = s_ref + r
    s_all = jnp.sum(s_all, axis=1, keepdims=True)
    s_ref = jnp.sum(s_ref, axis=1, keepdims=True)

    packed = jnp.where(lane == 0, m_all, jnp.zeros((R, 128), f32))
    packed = jnp.where(lane == 1, m_ref, packed)
    packed = jnp.where(lane == 8, s_all, packed)
    packed = jnp.where(lane == 9, s_ref, packed)
    packed = packed.T
    st1[j_own, 0] = packed[0:8]
    st1[j_own, 1] = packed[8:16]

    def spread_plane(buf):
        first = wires.used
        for d in range(1, NY * NC):
            wires.start(buf.at[j_own], buf.at[j_own], plane_by(d)[0])
        return first

    def await_plane(buf, first):
        for d in range(1, NY * NC):
            device, j = plane_by(NY * NC - d)
            wires.describe(buf.at[j], buf.at[j], device, first + d - 1).wait_recv()

    def spread_line(buf):
        first = wires.used
        for d in range(1, NZ):
            wires.start(buf.at[z], buf.at[z], z_by(d))
        return first

    def await_line(buf, first):
        for d in range(1, NZ):
            zz = (z + NZ - d) % NZ
            wires.describe(buf.at[zz], buf.at[zz], at(z_=zz), first + d - 1).wait_recv()

    def merged(buf, n):
        peak = buf[0, 0]
        for j in range(1, n):
            peak = jnp.maximum(peak, buf[j, 0])
        total = buf[0, 1] * jnp.exp(buf[0, 0] - peak)
        for j in range(1, n):
            total = total + buf[j, 1] * jnp.exp(buf[j, 0] - peak)
        return peak, total

    first = spread_plane(st1)
    await_plane(st1, first)
    peak, total = merged(st1, NY * NC)
    st2[z, 0] = peak
    st2[z, 1] = total
    first = spread_line(st2)
    await_line(st2, first)
    peak, total = merged(st2, NZ)
    row8 = lax.broadcasted_iota(jnp.int32, (8, 128), 0)
    lse = peak + jnp.log(jnp.where(row8 < 2, total, 1.0))
    log_ref[...] = lse[1:2] - lse[0:1]
    lse_cols = columns_of(lse)
    f_all = loss_col * jnp.exp(m_all - lse_cols[:, 0:1])
    f_ref = loss_col * jnp.exp(m_ref - lse_cols[:, 1:2])

    rt = jnp.zeros((R, T), f32)
    to_right, to_left = {}, {}
    def gather(t_r, t_l):
        to_right[t_r] = wires.start(gt.at[0, t_r], gt.at[3, t_r], right)
        to_left[t_l] = wires.start(gt.at[0, t_l], gt.at[1, t_l], left)

    for pair in ((0, 2), (1, 3)):
        for t in pair:
            g = (eref[t] * f_ref - eall[t] * f_all).astype(bf16)
            gt[0, t] = g
            rt = rt + g.astype(f32) * pown[t]
        gather(*pair)
    gather(2, 0)
    gather(3, 1)
    rt = jnp.sum(rt, axis=1, keepdims=True)
    rs1[j_own] = jnp.where(lane == 0, rt, jnp.zeros((R, 128), f32)).T[0:8]
    rt_first = spread_plane(rs1)

    def grad_tile(s, j, cc):
        yy = (y + j) % NY
        lhs = jnp.concatenate([gt[s, t] for t in range(VT)], axis=1)
        top = pl.multiple_of((yy * NC + cc) * 128, 128)
        low = pl.multiple_of(((NY + yy) * NC + cc) * 128, 128)
        rhs = jnp.concatenate([head[pl.ds(top, 128), :], head[pl.ds(low, 128), :]], axis=0)
        return lax.dot_general(
            lhs, rhs, (((1,), (1,)), ((), ())), preferred_element_type=f32
        )

    ccopy, yl2, yr2, yl, yr = {}, {}, {}, {}, {}
    up, down = y_by(1), y_by(NY - 1)

    def multiply(s):
        for j in (2, 1, 3, 0):
            csend[s, j] = grad_tile(s, j, 1 - c)
        ccopy[s] = wires.start(csend.at[s], crecv.at[s], sibling)
        for j in (2, 1, 3, 0):
            own32[s, j] = grad_tile(s, j, c)

    def y_first(s):
        ccopy[s].wait_recv()
        two = own32[s, 2] + crecv[s, 2]
        ytwo[s, 0] = two[:, :128].astype(bf16)
        ytwo[s, 1] = two[:, 128:].astype(bf16)
        yl2[s] = wires.start(ytwo.at[s, 0], yhl.at[s], up)
        yr2[s] = wires.start(ytwo.at[s, 1], yhr.at[s], down)
        one = own32[s, 1] + crecv[s, 1]
        own32[s, 1] = one
        yright[s, 1] = one[:, 128:].astype(bf16)
        yl[s, 1] = wires.start(yright.at[s, 1], yinl.at[s, 1], up)
        one = own32[s, 3] + crecv[s, 3]
        own32[s, 3] = one
        yleft[s, 0] = one[:, :128].astype(bf16)
        yr[s, 0] = wires.start(yleft.at[s, 0], yinr.at[s, 0], down)

    def y_second(s):
        yl2[s].wait_recv()
        yright[s, 0] = (own32[s, 1, :, :128] + yhl[s].astype(f32)).astype(bf16)
        yl[s, 0] = wires.start(yright.at[s, 0], yinl.at[s, 0], up)
        yr2[s].wait_recv()
        yleft[s, 1] = (own32[s, 3, :, 128:] + yhr[s].astype(f32)).astype(bf16)
        yr[s, 1] = wires.start(yleft.at[s, 1], yinr.at[s, 1], down)

    def place(s, zl):
        return pltpu.make_async_remote_copy(
            src_ref=fsend.at[s, zl],
            dst_ref=frecv.at[z],
            send_sem=fsend_sems.at[s * 2 + zl],
            recv_sem=frecv_sems.at[z],
            device_id=at(x_=(p + s) % NX, z_=2 * p + zl),
            device_id_type=pl.DeviceIdType.MESH,
        )

    def y_third(s):
        for zl in (1, 0):
            yl[s, zl].wait_recv()
            yr[s, zl].wait_recv()
            lanes = slice(zl * 128, zl * 128 + 128)
            out = own32[s, 0, :, lanes] + crecv[s, 0, :, lanes]
            out = out + yinl[s, zl].astype(f32) + yinr[s, zl].astype(f32)
            fsend[s, zl] = out
            if s:
                place(s, zl).start()
            else:

                @pl.when(z != 2 * p + zl)
                def _():
                    place(s, zl).start()

                @pl.when(z == 2 * p + zl)
                def _():
                    frecv[z] = fsend[s, zl]

    multiply(0)
    for t in (0, 1):
        to_right[t].wait_recv()
        wires.start(gt.at[3, t], gt.at[2, t], right)
        to_left[t + 2].wait_recv()
        wires.start(gt.at[1, t + 2], gt.at[2, t + 2], left)
    forward = wires.used - 4
    y_first(0)
    for t in (2, 3):
        to_right[t].wait_recv()
    multiply(3)
    y_second(0)
    for t in (0, 1):
        to_left[t].wait_recv()
    multiply(1)
    y_first(3)
    y_third(0)
    y_first(1)
    y_second(3)
    await_plane(rs1, rt_first)
    total = rs1[0]
    for j in range(1, NY * NC):
        total = total + rs1[j]
    rs2[z] = total
    rt_first = spread_line(rs2)
    for t in (0, 1):
        for i, tile, device in ((0, t, left), (1, t + 2, right)):
            wires.describe(
                gt.at[2, tile], gt.at[2, tile], device, forward + 2 * t + i
            ).wait_recv()
    multiply(2)
    y_second(1)
    y_third(3)
    y_first(2)
    y_third(1)
    y_second(2)
    await_line(rs2, rt_first)
    total = rs2[0]
    for j in range(1, NZ):
        total = total + rs2[j]
    rt_col = columns_of(total)[:, 0:1]
    y_third(2)

    own_cols = pl.ds(pl.multiple_of(v * 128, 128), 128)
    inv = inv_v[...]
    minus = hid[:, own_cols].astype(f32) * (inv * inv / 8192.0) * rt_col
    scale = inv * gain_ref[:, own_cols]
    for zs in range(NZ):

        @pl.when(jnp.logical_or(foreign, zs != z))
        def _():
            pltpu.make_async_remote_copy(
                src_ref=frecv.at[zs],
                dst_ref=frecv.at[zs],
                send_sem=fsend_sems.at[0],
                recv_sem=frecv_sems.at[zs],
                device_id=at(x_=source, z_=zs),
                device_id_type=pl.DeviceIdType.MESH,
            ).wait_recv()

    total = frecv[0]
    for zs in range(1, NZ):
        total = total + frecv[zs]
    grad_ref[...] = scale * total - minus

    wires.close()
    for s in range(NX):
        for zl in range(2):
            if s:
                place(s, zl).wait_send()
            else:

                @pl.when(z != 2 * p + zl)
                def _():
                    place(s, zl).wait_send()


def shards(hidden, head, gain, refusal_ids, refusal_count, loss_scale):
    V = pltpu.VMEM
    tile = (R, T)
    box = (R, 128)
    wires = 120
    grad, log_refusal = pl.pallas_call(
        kernel,
        out_shape=(
            jax.ShapeDtypeStruct((R, 128), f32),
            jax.ShapeDtypeStruct((1, R), f32),
        ),
        in_specs=[pl.BlockSpec(memory_space=pl.ANY)] * 2
        + [pl.BlockSpec(memory_space=pltpu.VMEM)] * 4,
        out_specs=(pl.BlockSpec(memory_space=pltpu.VMEM),) * 2,
        scratch_shapes=[
            V((R, NX * DL), bf16),
            V((DL, VL), bf16),
            V(box, f32),
            V((3, 4) + tile, bf16),
            V((NX, KT) + tile, bf16),
            V((VT,) + tile, f32),
            V((VT,) + tile, f32),
            V((VT,) + tile, f32),
            V((VT,) + tile, f32),
            V((2,) + tile, f32),
            V((2,) + tile, f32),
            V((VT,) + tile, f32),
            V((VT,) + tile, f32),
            V((VT,) + tile, jnp.int32),
            V((VT,) + tile, f32),
            V((VT,) + tile, f32),
            V((NY * NC, 2, 8, 128), f32),
            V((NZ, 2, 8, 128), f32),
            V((NY * NC, 8, 128), f32),
            V((NZ, 8, 128), f32),
            V((NX, VT) + tile, bf16),
            V((NX, NY) + tile, f32),
            V((NX, NY) + tile, f32),
            V((NX, NY) + tile, f32),
            V((NX, 2) + box, bf16),
            V((NX, 2) + box, bf16),
            V((NX, 2) + box, bf16),
            V((NX,) + box, bf16),
            V((NX,) + box, bf16),
            V((NX, 2) + box, bf16),
            V((NX, 2) + box, bf16),
            V((NX, 2) + box, f32),
            V((NZ,) + box, f32),
            pltpu.SemaphoreType.DMA((2,)),
            pltpu.SemaphoreType.DMA((wires,)),
            pltpu.SemaphoreType.DMA((wires,)),
            pltpu.SemaphoreType.DMA((NX * 2,)),
            pltpu.SemaphoreType.DMA((NZ,)),
        ],
        compiler_params=pltpu.CompilerParams(
            collective_id=0, has_side_effects=True, vmem_limit_bytes=48 << 20
        ),
        name="head_grad",
    )(
        hidden,
        head,
        gain.reshape(1, -1),
        refusal_ids,
        refusal_count.reshape(1, -1),
        loss_scale.reshape(1, -1),
    )
    return grad, log_refusal.reshape(-1)


def solution(mesh):
    return jax.shard_map(
        shards,
        mesh=mesh,
        in_specs=(
            P("prompt", None),
            P("prompt", "vocab"),
            P(),
            P("prompt", None),
            P("prompt"),
            P("prompt"),
        ),
        out_specs=(P("prompt", "vocab"), P("prompt")),
        check_vma=False,
    )
```

```python
import functools

import jax
import jax.numpy as jnp
from jax import lax
from jax.experimental import pallas as pl
from jax.experimental.pallas import tpu as pltpu
from jax.sharding import PartitionSpec as P

epsilon = 1e-05
lowest = -1e30
f32 = jnp.float32
bf16 = jnp.bfloat16

NX, NY, NZ, NC = 4, 4, 8, 2
R = 128
DL = 2048
VL = 1024
T = 256
KT = DL // T
VT = VL // T


class Wires:
    def __init__(self, send, recv):
        self.send, self.recv, self.used, self.open = send, recv, 0, []

    def describe(self, src, dst, device, index):
        return pltpu.make_async_remote_copy(
            src_ref=src,
            dst_ref=dst,
            send_sem=self.send.at[index],
            recv_sem=self.recv.at[index],
            device_id=device,
            device_id_type=pl.DeviceIdType.MESH,
        )

    def start(self, src, dst, device):
        copy = self.describe(src, dst, device, self.used)
        self.used += 1
        copy.start()
        self.open.append(copy)
        return copy

    def close(self):
        for copy in self.open:
            copy.wait_send()


def kernel(
    hid_hbm, head_hbm, gain_hbm, ids_hbm, count_hbm, loss_hbm, grad_ref, log_ref,
    hid, head, gain_ref, ids_ref, count_ref, loss_ref, inv_v, nsend, nrm, ptwo, pright, pleft, pown, hl, hr, inl, inr,
    mask, eall, eref, st1, st2, rs1, rs2, gt, csend, crecv, own32,
    ytwo, yright, yleft, yhl, yhr, yinl, yinr, fsend, xrecv, frecv,
    load_sems, send_sems, recv_sems, fsend_sems, frecv_sems,
):
    p = lax.axis_index("prompt")
    v = lax.axis_index("vocab")
    c = v % NC
    y = (v // NC) % NY
    z = v // (NC * NY)

    def at(x_=p, y_=y, z_=z, c_=c):
        return (x_, (z_ * NY + y_) * NC + c_)

    def x_by(d):
        return at(x_=(p + d) % NX)

    def y_by(d):
        return at(y_=(y + d) % NY)

    def z_by(d):
        return at(z_=(z + d) % NZ)

    j_own = y * NC + c

    def plane_by(d):
        j = (j_own + d) % (NY * NC)
        return at(y_=j // NC, c_=j % NC), j

    sibling = at(c_=1 - c)

    load_hid = pltpu.make_async_copy(hid_hbm, hid, load_sems.at[0])
    load_gain = pltpu.make_async_copy(gain_hbm, gain_ref, load_sems.at[1])
    load_head = pltpu.make_async_copy(head_hbm, head, load_sems.at[2])
    load_ids = pltpu.make_async_copy(ids_hbm, ids_ref, load_sems.at[3])
    load_count = pltpu.make_async_copy(count_hbm, count_ref, load_sems.at[4])
    load_loss = pltpu.make_async_copy(loss_hbm, loss_ref, load_sems.at[5])
    loads = (load_hid, load_gain, load_head, load_ids, load_count, load_loss)
    for load in loads:
        load.start()

    barrier = pltpu.get_barrier_semaphore()

    def greet(device):
        pl.semaphore_signal(
            barrier, inc=1, device_id=device, device_id_type=pl.DeviceIdType.MESH
        )

    for d in range(1, NX):
        greet(x_by(d))
    for d in range(1, NY * NC):
        greet(plane_by(d)[0])
    for d in range(1, NZ):
        greet(z_by(d))
    wires = Wires(send_sems, recv_sems)

    lane = lax.broadcasted_iota(jnp.int32, (R, 128), 1)
    sub = lax.broadcasted_iota(jnp.int32, (R, 128), 0)

    def columns_of(rows):
        return jnp.concatenate([rows, jnp.zeros((R - 8, 128), f32)], axis=0).T

    load_hid.wait()

    def square(j, acc):
        x = hid[:, pl.ds(pl.multiple_of(j * 1024, 1024), 1024)].astype(f32)
        x = x * x
        for i in range(8):
            acc = acc + x[:, i * 128 : (i + 1) * 128]
        return acc

    acc = lax.fori_loop(0, 8, square, jnp.zeros((R, 128), f32))
    inv = lax.rsqrt(jnp.sum(acc, axis=1, keepdims=True) / 8192.0 + epsilon)
    inv_v[...] = jnp.broadcast_to(inv, (R, 128))
    load_gain.wait()

    def normed(col):
        col = pl.multiple_of(col, T)
        x = hid[:, pl.ds(col, T)].astype(f32)
        return (x * inv * gain_ref[:, pl.ds(col, T)]).astype(bf16)

    k_own = c * NY + y
    for d in (2, 1, 3):
        nsend[d - 1] = normed((p + d) % NX * DL + k_own * T)

    pl.semaphore_wait(barrier, (NX - 1) + (NY * NC - 1) + (NZ - 1))

    up, down = y_by(1), y_by(NY - 1)
    near = {d: c * NY + (y + d) % NY for d in range(NY)}
    there = {d: (1 - c) * NY + (y + d) % NY for d in range(NY)}
    first_half, second_half = pl.ds(0, R // 2), pl.ds(R // 2, R // 2)
    come, go_up, go_down, far_up, far_down, shared = {}, {}, {}, {}, {}, {}
    for d in (2, 1, 3):
        slot = NX - d
        come[slot] = wires.start(nsend.at[d - 1], nrm.at[slot, k_own], x_by(d))
    for k in range(KT):
        nrm[0, k] = normed(p * DL + k * T)

    def share(slot, d):
        shared[slot, d] = wires.used
        wires.start(nrm.at[slot, near[d]], nrm.at[slot, near[d]], sibling)

    def arrived(slot, d, device, index, rows=None):
        piece = nrm.at[slot, near[d]] if rows is None else nrm.at[slot, near[d], rows]
        wires.describe(piece, piece, device, index).wait_recv()

    def near_out(slot):
        come[slot].wait_recv()
        piece = nrm.at[slot, k_own]
        go_up[slot] = wires.used
        wires.start(piece, piece, up)
        go_down[slot] = wires.used
        wires.start(piece, piece, down)
        share(slot, 0)

    def far_out(slot):
        arrived(slot, NY - 1, down, go_up[slot])
        piece = nrm.at[slot, near[NY - 1], first_half]
        far_up[slot] = wires.used
        wires.start(piece, piece, up)
        arrived(slot, 1, up, go_down[slot])
        piece = nrm.at[slot, near[1], second_half]
        far_down[slot] = wires.used
        wires.start(piece, piece, down)
        share(slot, NY - 1)
        share(slot, 1)

    def far_in(slot):
        arrived(slot, 2, down, far_up[slot], first_half)
        arrived(slot, 2, up, far_down[slot], second_half)
        share(slot, 2)

    def wait_share(slot):
        for d in range(NY):
            piece = nrm.at[slot, there[d]]
            wires.describe(piece, piece, sibling, shared[slot, d]).wait_recv()

    def partial(s, t):
        lhs = jnp.concatenate([nrm[s, k] for k in range(KT)], axis=1)
        return jnp.dot(lhs, head[:, t * T : (t + 1) * T], preferred_element_type=f32)

    right, left = x_by(1), x_by(NX - 1)
    near_out(2)
    near_out(3)
    near_out(1)
    far_out(2)
    far_in(2)
    far_out(3)
    far_out(1)
    load_head.wait()
    wait_share(2)
    ch_l, ch_r, cin_l, cin_r = {}, {}, {}, {}
    for t in (0, 2, 1, 3):
        ptwo[t] = partial(2, t)
        if t < 2:
            ch_l[t] = wires.start(ptwo.at[t], hl.at[t], right)
        else:
            ch_r[t - 2] = wires.start(ptwo.at[t], hr.at[t - 2], left)
    far_in(3)
    far_in(1)
    wait_share(1)
    for t in (2, 3):
        pright[t] = partial(1, t)
        cin_l[t] = wires.start(pright.at[t], inl.at[t], right)
    wait_share(3)
    for t in (0, 1):
        pleft[t] = partial(3, t)
        cin_r[t] = wires.start(pleft.at[t], inr.at[t], left)
    for t in (0, 1):
        pright[t] = partial(1, t)
        pleft[t + 2] = partial(3, t + 2)
    for t in (0, 1):
        ch_l[t].wait_recv()
        pright[t] = pright[t] + hl[t]
        cin_l[t] = wires.start(pright.at[t], inl.at[t], right)
        ch_r[t].wait_recv()
        pleft[t + 2] = pleft[t + 2] + hr[t]
        cin_r[t + 2] = wires.start(pleft.at[t + 2], inr.at[t + 2], left)
    for t in range(VT):
        pown[t] = partial(0, t)

    load_ids.wait()
    load_count.wait()
    load_loss.wait()
    ids = jnp.concatenate([ids_ref[...], jnp.zeros((R - 16, 128), jnp.int32)], axis=0).T
    cl = jnp.where(
        sub == 0,
        jnp.broadcast_to(count_ref[...].astype(f32), (R, 128)),
        jnp.where(sub == 1, jnp.broadcast_to(loss_ref[...], (R, 128)), 0.0),
    ).T
    count_col, loss_col = cl[:, 0:1], cl[:, 1:2]
    wide = lax.broadcasted_iota(jnp.int32, (R, T), 1)
    for t in range(VT):
        hit = jnp.zeros((R, T), jnp.int32)
        for k in range(16):
            here = ids[:, k : k + 1] - (v * VL + t * T)
            here = jnp.where(count_col > float(k), here, -1)
            hit = jnp.where(wide == here, 1, hit)
        mask[t] = hit

    m_all = jnp.full((R, T), -3e38, f32)
    m_ref = jnp.full((R, T), lowest, f32)
    for t in (2, 3, 0, 1):
        cin_l[t].wait_recv()
        cin_r[t].wait_recv()
        logit = pown[t] + inl[t] + inr[t]
        pown[t] = logit
        m_all = jnp.maximum(m_all, logit)
        m_ref = jnp.maximum(m_ref, jnp.where(mask[t] > 0, logit, lowest))
    m_all = jnp.max(m_all, axis=1, keepdims=True)
    m_ref = jnp.max(m_ref, axis=1, keepdims=True)
    s_all = jnp.zeros((R, T), f32)
    s_ref = jnp.zeros((R, T), f32)
    for t in range(VT):
        logit = pown[t]
        e = jnp.exp(logit - m_all)
        r = jnp.exp(jnp.where(mask[t] > 0, logit - m_ref, lowest))
        eall[t] = e
        eref[t] = r
        s_all = s_all + e
        s_ref = s_ref + r
    s_all = jnp.sum(s_all, axis=1, keepdims=True)
    s_ref = jnp.sum(s_ref, axis=1, keepdims=True)

    packed = jnp.where(lane == 0, m_all, jnp.zeros((R, 128), f32))
    packed = jnp.where(lane == 1, m_ref, packed)
    packed = jnp.where(lane == 8, s_all, packed)
    packed = jnp.where(lane == 9, s_ref, packed)
    packed = packed.T
    st1[j_own, 0] = packed[0:8]
    st1[j_own, 1] = packed[8:16]

    def spread_plane(buf):
        first = wires.used
        for d in range(1, NY * NC):
            wires.start(buf.at[j_own], buf.at[j_own], plane_by(d)[0])
        return first

    def await_plane(buf, first):
        for d in range(1, NY * NC):
            device, j = plane_by(NY * NC - d)
            wires.describe(buf.at[j], buf.at[j], device, first + d - 1).wait_recv()

    def spread_line(buf):
        first = wires.used
        for d in range(1, NZ):
            wires.start(buf.at[z], buf.at[z], z_by(d))
        return first

    def await_line(buf, first):
        for d in range(1, NZ):
            zz = (z + NZ - d) % NZ
            wires.describe(buf.at[zz], buf.at[zz], at(z_=zz), first + d - 1).wait_recv()

    def merged(buf, n):
        peak = buf[0, 0]
        for j in range(1, n):
            peak = jnp.maximum(peak, buf[j, 0])
        total = buf[0, 1] * jnp.exp(buf[0, 0] - peak)
        for j in range(1, n):
            total = total + buf[j, 1] * jnp.exp(buf[j, 0] - peak)
        return peak, total

    first = spread_plane(st1)
    await_plane(st1, first)
    peak, total = merged(st1, NY * NC)
    st2[z, 0] = peak
    st2[z, 1] = total
    first = spread_line(st2)
    await_line(st2, first)
    peak, total = merged(st2, NZ)
    row8 = lax.broadcasted_iota(jnp.int32, (8, 128), 0)
    lse = peak + jnp.log(jnp.where(row8 < 2, total, 1.0))
    log_ref[...] = lse[1:2] - lse[0:1]
    lse_cols = columns_of(lse)
    f_all = loss_col * jnp.exp(m_all - lse_cols[:, 0:1])
    f_ref = loss_col * jnp.exp(m_ref - lse_cols[:, 1:2])

    rt = jnp.zeros((R, T), f32)
    to_right, to_left = {}, {}
    def gather(t_r, t_l):
        to_right[t_r] = wires.start(gt.at[0, t_r], gt.at[3, t_r], right)
        to_left[t_l] = wires.start(gt.at[0, t_l], gt.at[1, t_l], left)

    for pair in ((0, 2), (1, 3)):
        for t in pair:
            g = eref[t] * f_ref - eall[t] * f_all
            gt[0, t] = g.T.astype(bf16)
            rt = rt + g.astype(bf16).astype(f32) * pown[t]
        gather(*pair)
    gather(2, 0)
    gather(3, 1)
    rt = jnp.sum(rt, axis=1, keepdims=True)
    rs1[j_own] = jnp.where(lane == 0, rt, jnp.zeros((R, 128), f32)).T[0:8]
    rt_first = spread_plane(rs1)

    def grad_block(s, zl, cc):
        rows = [
            pl.multiple_of(((zl * NY + yy) * NC + cc) * 128, 128) for yy in range(NY)
        ]
        lhs = jnp.concatenate([head[pl.ds(row, 128), :] for row in rows], axis=0)
        rhs = jnp.concatenate([gt[s, t] for t in range(VT)], axis=0)
        out = jnp.dot(lhs, rhs, preferred_element_type=f32)
        return out.reshape(NY, 128, R)

    ccopy, yl2, yr2, yl, yr = {}, {}, {}, {}, {}
    y1, y2, y3 = ((y + d) % NY for d in (1, 2, 3))

    def multiply(s):
        for zl in range(2):
            csend[s, zl] = grad_block(s, zl, 1 - c)
            ccopy[s, zl] = wires.start(csend.at[s, zl], crecv.at[s, zl], sibling)
        for zl in range(2):
            own32[s, zl] = grad_block(s, zl, c)

    def pair_sum(s, zl, yy):
        return own32[s, zl, yy] + crecv[s, zl, yy]

    def y_first(s):
        for zl in range(2):
            ccopy[s, zl].wait_recv()
            ytwo[s, zl] = pair_sum(s, zl, y2).astype(bf16)
        yl2[s] = wires.start(ytwo.at[s, 0], yhl.at[s], up)
        yr2[s] = wires.start(ytwo.at[s, 1], yhr.at[s], down)
        yright[s, 1] = pair_sum(s, 1, y1).astype(bf16)
        yl[s, 1] = wires.start(yright.at[s, 1], yinl.at[s, 1], up)
        yleft[s, 0] = pair_sum(s, 0, y3).astype(bf16)
        yr[s, 0] = wires.start(yleft.at[s, 0], yinr.at[s, 0], down)

    def y_second(s):
        yl2[s].wait_recv()
        yright[s, 0] = (pair_sum(s, 0, y1) + yhl[s].astype(f32)).astype(bf16)
        yl[s, 0] = wires.start(yright.at[s, 0], yinl.at[s, 0], up)
        yr2[s].wait_recv()
        yleft[s, 1] = (pair_sum(s, 1, y3) + yhr[s].astype(f32)).astype(bf16)
        yr[s, 1] = wires.start(yleft.at[s, 1], yinr.at[s, 1], down)

    def place(s, zl):
        return pltpu.make_async_remote_copy(
            src_ref=xrecv.at[s, zl],
            dst_ref=frecv.at[z],
            send_sem=fsend_sems.at[s * 2 + zl],
            recv_sem=frecv_sems.at[z],
            device_id=at(z_=(p + NX - s) % NX * 2 + zl),
            device_id_type=pl.DeviceIdType.MESH,
        )

    move = {}

    def y_third(s):
        for zl in (1, 0):
            yl[s, zl].wait_recv()
            yr[s, zl].wait_recv()
            out = pair_sum(s, zl, y)
            out = out + yinl[s, zl].astype(f32) + yinr[s, zl].astype(f32)
            if s:
                fsend[s, zl] = out.astype(bf16)
                move[s, zl] = wires.start(fsend.at[s, zl], xrecv.at[s, zl], x_by(s))
            else:
                xrecv[s, zl] = out.astype(bf16)

    def z_out(s):
        for zl in (1, 0):
            if s:
                move[s, zl].wait_recv()
            there_z = (p + NX - s) % NX * 2 + zl

            @pl.when(z != there_z)
            def _():
                place(s, zl).start()

            @pl.when(z == there_z)
            def _():
                frecv[z] = xrecv[s, zl]

    multiply(0)
    for t in (0, 1):
        to_right[t].wait_recv()
        wires.start(gt.at[3, t], gt.at[2, t], right)
        to_left[t + 2].wait_recv()
        wires.start(gt.at[1, t + 2], gt.at[2, t + 2], left)
    forward = wires.used - 4
    y_first(0)
    for t in (2, 3):
        to_right[t].wait_recv()
    multiply(3)
    y_second(0)
    for t in (0, 1):
        to_left[t].wait_recv()
    multiply(1)
    y_first(3)
    y_third(0)
    z_out(0)
    y_first(1)
    y_second(3)
    await_plane(rs1, rt_first)
    total = rs1[0]
    for j in range(1, NY * NC):
        total = total + rs1[j]
    rs2[z] = total
    rt_first = spread_line(rs2)
    for t in (0, 1):
        for i, tile, device in ((0, t, left), (1, t + 2, right)):
            wires.describe(
                gt.at[2, tile], gt.at[2, tile], device, forward + 2 * t + i
            ).wait_recv()
    multiply(2)
    y_second(1)
    y_third(3)
    y_first(2)
    y_third(1)
    z_out(3)
    y_second(2)
    z_out(1)
    await_line(rs2, rt_first)
    total = rs2[0]
    for j in range(1, NZ):
        total = total + rs2[j]
    rt_col = columns_of(total)[:, 0:1]
    y_third(2)
    z_out(2)

    own_cols = pl.ds(pl.multiple_of(v * 128, 128), 128)
    inv = inv_v[...]
    minus = hid[:, own_cols].astype(f32) * (inv * inv / 8192.0) * rt_col
    scale = inv * gain_ref[:, own_cols]
    for zs in range(NZ):

        @pl.when(zs != z)
        def _():
            pltpu.make_async_remote_copy(
                src_ref=frecv.at[zs],
                dst_ref=frecv.at[zs],
                send_sem=fsend_sems.at[0],
                recv_sem=frecv_sems.at[zs],
                device_id=at(z_=zs),
                device_id_type=pl.DeviceIdType.MESH,
            ).wait_recv()

    total = frecv[0].astype(f32)
    for zs in range(1, NZ):
        total = total + frecv[zs].astype(f32)
    grad_ref[...] = scale * total.T - minus

    wires.close()
    for s in range(NX):
        for zl in range(2):

            @pl.when(z != (p + NX - s) % NX * 2 + zl)
            def _():
                place(s, zl).wait_send()


def shards(hidden, head, gain, refusal_ids, refusal_count, loss_scale):
    V = pltpu.VMEM
    tile = (R, T)
    box = (R, 128)
    wires = 140
    grad, log_refusal = pl.pallas_call(
        kernel,
        out_shape=(
            jax.ShapeDtypeStruct((R, 128), f32),
            jax.ShapeDtypeStruct((1, R), f32),
        ),
        in_specs=[pl.BlockSpec(memory_space=pltpu.HBM)] * 6,
        out_specs=(pl.BlockSpec(memory_space=pltpu.VMEM),) * 2,
        scratch_shapes=[
            V((R, NX * DL), bf16),
            V((DL, VL), bf16),
            V((1, NX * DL), f32),
            V((16, R), jnp.int32),
            V((1, R), jnp.int32),
            V((1, R), f32),
            V(box, f32),
            V((3,) + tile, bf16),
            V((NX, KT) + tile, bf16),
            V((VT,) + tile, f32),
            V((VT,) + tile, f32),
            V((VT,) + tile, f32),
            V((VT,) + tile, f32),
            V((2,) + tile, f32),
            V((2,) + tile, f32),
            V((VT,) + tile, f32),
            V((VT,) + tile, f32),
            V((VT,) + tile, jnp.int32),
            V((VT,) + tile, f32),
            V((VT,) + tile, f32),
            V((NY * NC, 2, 8, 128), f32),
            V((NZ, 2, 8, 128), f32),
            V((NY * NC, 8, 128), f32),
            V((NZ, 8, 128), f32),
            V((NX, VT, T, R), bf16),
            V((NX, 2, NY) + box, f32),
            V((NX, 2, NY) + box, f32),
            V((NX, 2, NY) + box, f32),
            V((NX, 2) + box, bf16),
            V((NX, 2) + box, bf16),
            V((NX, 2) + box, bf16),
            V((NX,) + box, bf16),
            V((NX,) + box, bf16),
            V((NX, 2) + box, bf16),
            V((NX, 2) + box, bf16),
            V((NX, 2) + box, bf16),
            V((NX, 2) + box, bf16),
            V((NZ,) + box, bf16),
            pltpu.SemaphoreType.DMA((6,)),
            pltpu.SemaphoreType.DMA((wires,)),
            pltpu.SemaphoreType.DMA((wires,)),
            pltpu.SemaphoreType.DMA((NX * 2,)),
            pltpu.SemaphoreType.DMA((NZ,)),
        ],
        compiler_params=pltpu.CompilerParams(
            collective_id=0, has_side_effects=True, vmem_limit_bytes=63 << 20
        ),
        name="head_grad",
    )(
        hidden,
        head,
        gain.reshape(1, -1),
        refusal_ids.T,
        refusal_count.reshape(1, -1),
        loss_scale.reshape(1, -1),
    )
    return grad, log_refusal.reshape(-1)


def solution(mesh):
    return jax.shard_map(
        shards,
        mesh=mesh,
        in_specs=(
            P("prompt", None),
            P("prompt", "vocab"),
            P(),
            P("prompt", None),
            P("prompt"),
            P("prompt"),
        ),
        out_specs=(P("prompt", "vocab"), P("prompt")),
        check_vma=False,
    )
```

```python
import functools

import jax
import jax.numpy as jnp
from jax import lax
from jax.experimental import pallas as pl
from jax.experimental.pallas import tpu as pltpu
from jax.sharding import PartitionSpec as P

epsilon = 1e-05
lowest = -1e30
f32 = jnp.float32
bf16 = jnp.bfloat16

NX, NY, NZ, NC = 4, 4, 8, 2
R = 128
DL = 2048
VL = 1024
T = 256
KT = DL // T
VT = VL // T


class Wires:
    def __init__(self, send, recv):
        self.send, self.recv, self.used, self.open = send, recv, 0, []

    def describe(self, src, dst, device, index):
        return pltpu.make_async_remote_copy(
            src_ref=src,
            dst_ref=dst,
            send_sem=self.send.at[index],
            recv_sem=self.recv.at[index],
            device_id=device,
            device_id_type=pl.DeviceIdType.MESH,
        )

    def start(self, src, dst, device):
        copy = self.describe(src, dst, device, self.used)
        self.used += 1
        copy.start()
        self.open.append(copy)
        return copy

    def close(self):
        for copy in self.open:
            copy.wait_send()


def kernel(
    hid_hbm, head_hbm, gain_hbm, ids_hbm, count_hbm, loss_hbm, grad_ref, log_ref,
    hid, head, gain_ref, ids_ref, count_ref, loss_ref, inv_v, nfar, nsend, nrm, ptwo, pright, pleft, pown, hl, hr, inl, inr,
    mask, eall, eref, st1, st2, rs1, rs2, gt, gs, lent, own32,
    ytwo, yright, yleft, yhl, yhr, yinl, yinr, fsend, xrecv, frecv,
    load_sems, send_sems, recv_sems, fsend_sems, frecv_sems,
):
    p = lax.axis_index("prompt")
    v = lax.axis_index("vocab")
    c = v % NC
    y = (v // NC) % NY
    z = v // (NC * NY)

    def at(x_=p, y_=y, z_=z, c_=c):
        return (x_, (z_ * NY + y_) * NC + c_)

    def x_by(d):
        return at(x_=(p + d) % NX)

    def y_by(d):
        return at(y_=(y + d) % NY)

    def z_by(d):
        return at(z_=(z + d) % NZ)

    j_own = y * NC + c

    def plane_by(d):
        j = (j_own + d) % (NY * NC)
        return at(y_=j // NC, c_=j % NC), j

    sibling = at(c_=1 - c)

    load_hid = pltpu.make_async_copy(hid_hbm, hid, load_sems.at[0])
    load_gain = pltpu.make_async_copy(gain_hbm, gain_ref, load_sems.at[1])
    load_head = pltpu.make_async_copy(head_hbm, head, load_sems.at[2])
    load_ids = pltpu.make_async_copy(ids_hbm, ids_ref, load_sems.at[3])
    load_count = pltpu.make_async_copy(count_hbm, count_ref, load_sems.at[4])
    load_loss = pltpu.make_async_copy(loss_hbm, loss_ref, load_sems.at[5])
    loads = (load_hid, load_gain, load_head, load_ids, load_count, load_loss)
    for load in loads:
        load.start()

    barrier = pltpu.get_barrier_semaphore()

    def greet(device):
        pl.semaphore_signal(
            barrier, inc=1, device_id=device, device_id_type=pl.DeviceIdType.MESH
        )

    for d in range(1, NX):
        greet(x_by(d))
    for d in range(1, NY * NC):
        greet(plane_by(d)[0])
    for d in range(1, NZ):
        greet(z_by(d))
    wires = Wires(send_sems, recv_sems)

    lane = lax.broadcasted_iota(jnp.int32, (R, 128), 1)
    sub = lax.broadcasted_iota(jnp.int32, (R, 128), 0)

    def columns_of(rows):
        return jnp.concatenate([rows, jnp.zeros((R - 8, 128), f32)], axis=0).T

    load_hid.wait()

    def square(j, acc):
        x = hid[:, pl.ds(pl.multiple_of(j * 1024, 1024), 1024)].astype(f32)
        x = x * x
        for i in range(8):
            acc = acc + x[:, i * 128 : (i + 1) * 128]
        return acc

    acc = lax.fori_loop(0, 8, square, jnp.zeros((R, 128), f32))
    inv = lax.rsqrt(jnp.sum(acc, axis=1, keepdims=True) / 8192.0 + epsilon)
    inv_v[...] = jnp.broadcast_to(inv, (R, 128))
    load_gain.wait()

    def normed(col):
        col = pl.multiple_of(col, T)
        x = hid[:, pl.ds(col, T)].astype(f32)
        return (x * inv * gain_ref[:, pl.ds(col, T)]).astype(bf16)

    near = {d: c * NY + (y + d) % NY for d in range(NY)}
    nfar[...] = normed((p + 2) % NX * DL + near[0] * T)

    pl.semaphore_wait(barrier, (NX - 1) + (NY * NC - 1) + (NZ - 1))

    up, down = y_by(1), y_by(NY - 1)
    right, left = x_by(1), x_by(NX - 1)
    half, other_half = pl.ds(c * NY, NY), pl.ds((1 - c) * NY, NY)
    come2 = wires.start(nfar, nrm.at[2, near[0]], x_by(2))
    come, shared = {}, {}
    for slot, i, device, d in ((3, 0, right, 1), (1, 1, left, NX - 1)):
        for k in range(NY):
            nsend[i, k] = normed((p + d) % NX * DL + (c * NY + k) * T)
        come[slot] = wires.start(nsend.at[i], nrm.at[slot, half], device)

    def piece(d):
        return nrm.at[2, near[d]]

    come2.wait_recv()
    for d in (1, 3, 2):
        wires.start(piece(0), piece(0), y_by(NY - d))
    shared[0] = wires.start(piece(0), piece(0), sibling)
    spread_at = dict(zip((1, 3, 2), range(wires.used - 4, wires.used - 1)))
    for k in range(KT):
        nrm[0, k] = normed(p * DL + k * T)
    for d in (1, 3, 2):
        wires.describe(piece(d), piece(d), y_by(d), spread_at[d]).wait_recv()
        shared[d] = wires.start(piece(d), piece(d), sibling)
    shared_at = dict(zip((0, 1, 3, 2), (wires.used - 4, *range(wires.used - 3, wires.used))))

    def share(slot):
        come[slot].wait_recv()
        rows = nrm.at[slot, half]
        shared[slot, "at"] = wires.used
        wires.start(rows, rows, sibling)

    def wait_share(slot):
        if slot == 2:
            for d in range(NY):
                rows = nrm.at[2, (1 - c) * NY + (y + d) % NY]
                wires.describe(rows, rows, sibling, shared_at[d]).wait_recv()
        else:
            rows = nrm.at[slot, other_half]
            wires.describe(rows, rows, sibling, shared[slot, "at"]).wait_recv()

    def partial(s, t):
        lhs = jnp.concatenate([nrm[s, k] for k in range(KT)], axis=1)
        return jnp.dot(lhs, head[:, t * T : (t + 1) * T], preferred_element_type=f32)

    load_head.wait()
    wait_share(2)
    ch_l, ch_r, cin_l, cin_r = {}, {}, {}, {}
    for t in (0, 2, 1, 3):
        ptwo[t] = partial(2, t)
        if t < 2:
            ch_l[t] = wires.start(ptwo.at[t], hl.at[t], right)
        else:
            ch_r[t - 2] = wires.start(ptwo.at[t], hr.at[t - 2], left)
    share(3)
    share(1)
    wait_share(1)
    for t in (2, 3):
        pright[t] = partial(1, t)
        cin_l[t] = wires.start(pright.at[t], inl.at[t], right)
    wait_share(3)
    for t in (0, 1):
        pleft[t] = partial(3, t)
        cin_r[t] = wires.start(pleft.at[t], inr.at[t], left)
    for t in (0, 1):
        pright[t] = partial(1, t)
        pleft[t + 2] = partial(3, t + 2)
    for t in (0, 1):
        ch_l[t].wait_recv()
        pright[t] = pright[t] + hl[t]
        cin_l[t] = wires.start(pright.at[t], inl.at[t], right)
        ch_r[t].wait_recv()
        pleft[t + 2] = pleft[t + 2] + hr[t]
        cin_r[t + 2] = wires.start(pleft.at[t + 2], inr.at[t + 2], left)
    lend = {}
    for b in range(2 * NY):
        rows = pl.ds(pl.multiple_of((b * NC + 1 - c) * 128, 128), 128)
        lend[b] = wires.start(head.at[rows], lent.at[b], sibling)
    for t in range(VT):
        pown[t] = partial(0, t)

    load_ids.wait()
    load_count.wait()
    load_loss.wait()
    ids = jnp.concatenate([ids_ref[...], jnp.zeros((R - 16, 128), jnp.int32)], axis=0).T
    cl = jnp.where(
        sub == 0,
        jnp.broadcast_to(count_ref[...].astype(f32), (R, 128)),
        jnp.where(sub == 1, jnp.broadcast_to(loss_ref[...], (R, 128)), 0.0),
    ).T
    count_col, loss_col = cl[:, 0:1], cl[:, 1:2]
    wide = lax.broadcasted_iota(jnp.int32, (R, T), 1)
    for t in range(VT):
        hit = jnp.zeros((R, T), jnp.int32)
        for k in range(16):
            here = ids[:, k : k + 1] - (v * VL + t * T)
            here = jnp.where(count_col > float(k), here, -1)
            hit = jnp.where(wide == here, 1, hit)
        mask[t] = hit

    m_all = jnp.full((R, T), -3e38, f32)
    m_ref = jnp.full((R, T), lowest, f32)
    for t in (2, 3, 0, 1):
        cin_l[t].wait_recv()
        cin_r[t].wait_recv()
        logit = pown[t] + inl[t] + inr[t]
        pown[t] = logit
        m_all = jnp.maximum(m_all, logit)
        m_ref = jnp.maximum(m_ref, jnp.where(mask[t] > 0, logit, lowest))
    m_all = jnp.max(m_all, axis=1, keepdims=True)
    m_ref = jnp.max(m_ref, axis=1, keepdims=True)
    s_all = jnp.zeros((R, T), f32)
    s_ref = jnp.zeros((R, T), f32)
    for t in range(VT):
        logit = pown[t]
        e = jnp.exp(logit - m_all)
        r = jnp.exp(jnp.where(mask[t] > 0, logit - m_ref, lowest))
        eall[t] = e
        eref[t] = r
        s_all = s_all + e
        s_ref = s_ref + r
    s_all = jnp.sum(s_all, axis=1, keepdims=True)
    s_ref = jnp.sum(s_ref, axis=1, keepdims=True)

    packed = jnp.where(lane == 0, m_all, jnp.zeros((R, 128), f32))
    packed = jnp.where(lane == 1, m_ref, packed)
    packed = jnp.where(lane == 8, s_all, packed)
    packed = jnp.where(lane == 9, s_ref, packed)
    packed = packed.T
    st1[j_own, 0] = packed[0:8]
    st1[j_own, 1] = packed[8:16]

    def spread_plane(buf):
        first = wires.used
        for d in range(1, NY * NC):
            wires.start(buf.at[j_own], buf.at[j_own], plane_by(d)[0])
        return first

    def await_plane(buf, first):
        for d in range(1, NY * NC):
            device, j = plane_by(NY * NC - d)
            wires.describe(buf.at[j], buf.at[j], device, first + d - 1).wait_recv()

    def spread_line(buf):
        first = wires.used
        for d in range(1, NZ):
            wires.start(buf.at[z], buf.at[z], z_by(d))
        return first

    def await_line(buf, first):
        for d in range(1, NZ):
            zz = (z + NZ - d) % NZ
            wires.describe(buf.at[zz], buf.at[zz], at(z_=zz), first + d - 1).wait_recv()

    def merged(buf, n):
        peak = buf[0, 0]
        for j in range(1, n):
            peak = jnp.maximum(peak, buf[j, 0])
        total = buf[0, 1] * jnp.exp(buf[0, 0] - peak)
        for j in range(1, n):
            total = total + buf[j, 1] * jnp.exp(buf[j, 0] - peak)
        return peak, total

    first = spread_plane(st1)
    await_plane(st1, first)
    peak, total = merged(st1, NY * NC)
    st2[z, 0] = peak
    st2[z, 1] = total
    first = spread_line(st2)
    await_line(st2, first)
    peak, total = merged(st2, NZ)
    row8 = lax.broadcasted_iota(jnp.int32, (8, 128), 0)
    lse = peak + jnp.log(jnp.where(row8 < 2, total, 1.0))
    log_ref[...] = lse[1:2] - lse[0:1]
    lse_cols = columns_of(lse)
    f_all = loss_col * jnp.exp(m_all - lse_cols[:, 0:1])
    f_ref = loss_col * jnp.exp(m_ref - lse_cols[:, 1:2])

    rt = jnp.zeros((R, T), f32)
    to_right, to_left = {}, {}
    def gather(t_r, t_l):
        to_right[t_r] = wires.start(gt.at[0, t_r], gt.at[3, t_r], right)
        to_left[t_l] = wires.start(gt.at[0, t_l], gt.at[1, t_l], left)

    for pair in ((0, 2), (1, 3)):
        for t in pair:
            g = eref[t] * f_ref - eall[t] * f_all
            g = g.astype(bf16)
            gt[0, t] = g
            rt = rt + g.astype(f32) * pown[t]
        gather(*pair)
    gather(2, 0)
    gather(3, 1)
    lot = {}

    def to_sibling(s, t):
        lot[s, t] = wires.start(gt.at[s, t], gs.at[s, t], sibling)

    for t in (0, 2, 1, 3):
        to_sibling(0, t)
    rt = jnp.sum(rt, axis=1, keepdims=True)
    rs1[j_own] = jnp.where(lane == 0, rt, jnp.zeros((R, 128), f32)).T[0:8]
    rt_first = spread_plane(rs1)

    yl2, yr2, yl, yr = {}, {}, {}, {}
    y1, y2, y3 = ((y + d) % NY for d in (1, 2, 3))

    def multiply(s):
        for t in range(VT):
            lot[s, t].wait_recv()
        mine = jnp.concatenate([gt[s, t] for t in range(VT)], axis=1)
        other = jnp.concatenate([gs[s, t] for t in range(VT)], axis=1)
        for zl in range(2):
            rows = [
                pl.multiple_of(((zl * NY + yy) * NC + c) * 128, 128)
                for yy in range(NY)
            ]
            here = jnp.concatenate([head[pl.ds(row, 128), :] for row in rows], axis=0)
            from_lent = lent[zl * NY : (zl + 1) * NY].reshape(NY * 128, VL)
            out = jnp.dot(here, mine.T, preferred_element_type=f32)
            out = out + jnp.dot(from_lent, other.T, preferred_element_type=f32)
            own32[s, zl] = out.reshape(NY, 128, R)

    def y_first(s):
        for zl in range(2):
            ytwo[s, zl] = own32[s, zl, y2].astype(bf16)
        yl2[s] = wires.start(ytwo.at[s, 0], yhl.at[s], up)
        yr2[s] = wires.start(ytwo.at[s, 1], yhr.at[s], down)
        yright[s, 1] = own32[s, 1, y1].astype(bf16)
        yl[s, 1] = wires.start(yright.at[s, 1], yinl.at[s, 1], up)
        yleft[s, 0] = own32[s, 0, y3].astype(bf16)
        yr[s, 0] = wires.start(yleft.at[s, 0], yinr.at[s, 0], down)

    def y_second(s):
        yl2[s].wait_recv()
        yright[s, 0] = (own32[s, 0, y1] + yhl[s].astype(f32)).astype(bf16)
        yl[s, 0] = wires.start(yright.at[s, 0], yinl.at[s, 0], up)
        yr2[s].wait_recv()
        yleft[s, 1] = (own32[s, 1, y3] + yhr[s].astype(f32)).astype(bf16)
        yr[s, 1] = wires.start(yleft.at[s, 1], yinr.at[s, 1], down)

    def place(s, zl):
        return pltpu.make_async_remote_copy(
            src_ref=xrecv.at[s, zl],
            dst_ref=frecv.at[z],
            send_sem=fsend_sems.at[s * 2 + zl],
            recv_sem=frecv_sems.at[z],
            device_id=at(z_=(p + NX - s) % NX * 2 + zl),
            device_id_type=pl.DeviceIdType.MESH,
        )

    move = {}

    def y_third(s):
        for zl in (1, 0):
            yl[s, zl].wait_recv()
            yr[s, zl].wait_recv()
            out = own32[s, zl, y]
            out = out + yinl[s, zl].astype(f32) + yinr[s, zl].astype(f32)
            if s:
                fsend[s, zl] = out.astype(bf16)
                move[s, zl] = wires.start(fsend.at[s, zl], xrecv.at[s, zl], x_by(s))
            else:
                xrecv[s, zl] = out.astype(bf16)

    def z_out(s):
        for zl in (1, 0):
            if s:
                move[s, zl].wait_recv()
            there_z = (p + NX - s) % NX * 2 + zl

            @pl.when(z != there_z)
            def _():
                place(s, zl).start()

            @pl.when(z == there_z)
            def _():
                frecv[z] = xrecv[s, zl]

    for b in range(2 * NY):
        lend[b].wait_recv()
    multiply(0)
    for t in (0, 1):
        to_right[t].wait_recv()
        wires.start(gt.at[3, t], gt.at[2, t], right)
        to_left[t + 2].wait_recv()
        wires.start(gt.at[1, t + 2], gt.at[2, t + 2], left)
        to_sibling(3, t)
        to_sibling(1, t + 2)
    forward = wires.used - 8
    y_first(0)
    for t in (2, 3):
        to_right[t].wait_recv()
        to_sibling(3, t)
        to_left[t - 2].wait_recv()
        to_sibling(1, t - 2)
    y_second(0)
    multiply(3)
    y_first(3)
    multiply(1)
    y_first(1)
    y_third(0)
    z_out(0)
    for t in (0, 1):
        for i, tile, device in ((0, t, left), (1, t + 2, right)):
            wires.describe(
                gt.at[2, tile], gt.at[2, tile], device, forward + 4 * t + i
            ).wait_recv()
            to_sibling(2, tile)
    multiply(2)
    y_first(2)
    await_plane(rs1, rt_first)
    total = rs1[0]
    for j in range(1, NY * NC):
        total = total + rs1[j]
    rs2[z] = total
    rt_first = spread_line(rs2)
    y_second(3)
    y_second(1)
    y_second(2)
    y_third(3)
    y_third(1)
    y_third(2)
    z_out(3)
    z_out(1)
    await_line(rs2, rt_first)
    total = rs2[0]
    for j in range(1, NZ):
        total = total + rs2[j]
    rt_col = columns_of(total)[:, 0:1]
    z_out(2)

    own_cols = pl.ds(pl.multiple_of(v * 128, 128), 128)
    inv = inv_v[...]
    minus = hid[:, own_cols].astype(f32) * (inv * inv / 8192.0) * rt_col
    scale = inv * gain_ref[:, own_cols]
    for zs in range(NZ):

        @pl.when(zs != z)
        def _():
            pltpu.make_async_remote_copy(
                src_ref=frecv.at[zs],
                dst_ref=frecv.at[zs],
                send_sem=fsend_sems.at[0],
                recv_sem=frecv_sems.at[zs],
                device_id=at(z_=zs),
                device_id_type=pl.DeviceIdType.MESH,
            ).wait_recv()

    total = frecv[0].astype(f32)
    for zs in range(1, NZ):
        total = total + frecv[zs].astype(f32)
    grad_ref[...] = scale * total.T - minus

    wires.close()
    for s in range(NX):
        for zl in range(2):

            @pl.when(z != (p + NX - s) % NX * 2 + zl)
            def _():
                place(s, zl).wait_send()


def shards(hidden, head, gain, refusal_ids, refusal_count, loss_scale):
    V = pltpu.VMEM
    tile = (R, T)
    box = (R, 128)
    wires = 140
    grad, log_refusal = pl.pallas_call(
        kernel,
        out_shape=(
            jax.ShapeDtypeStruct((R, 128), f32),
            jax.ShapeDtypeStruct((1, R), f32),
        ),
        in_specs=[pl.BlockSpec(memory_space=pltpu.HBM)] * 6,
        out_specs=(pl.BlockSpec(memory_space=pltpu.VMEM),) * 2,
        scratch_shapes=[
            V((R, NX * DL), bf16),
            V((DL, VL), bf16),
            V((1, NX * DL), f32),
            V((16, R), jnp.int32),
            V((1, R), jnp.int32),
            V((1, R), f32),
            V(box, f32),
            V(tile, bf16),
            V((2, NY) + tile, bf16),
            V((NX, KT) + tile, bf16),
            V((VT,) + tile, f32),
            V((VT,) + tile, f32),
            V((VT,) + tile, f32),
            V((VT,) + tile, f32),
            V((2,) + tile, f32),
            V((2,) + tile, f32),
            V((VT,) + tile, f32),
            V((VT,) + tile, f32),
            V((VT,) + tile, jnp.int32),
            V((VT,) + tile, f32),
            V((VT,) + tile, f32),
            V((NY * NC, 2, 8, 128), f32),
            V((NZ, 2, 8, 128), f32),
            V((NY * NC, 8, 128), f32),
            V((NZ, 8, 128), f32),
            V((NX, VT) + tile, bf16),
            V((NX, VT) + tile, bf16),
            V((2 * NY, 128, VL), bf16),
            V((NX, 2, NY) + box, f32),
            V((NX, 2) + box, bf16),
            V((NX, 2) + box, bf16),
            V((NX, 2) + box, bf16),
            V((NX,) + box, bf16),
            V((NX,) + box, bf16),
            V((NX, 2) + box, bf16),
            V((NX, 2) + box, bf16),
            V((NX, 2) + box, bf16),
            V((NX, 2) + box, bf16),
            V((NZ,) + box, bf16),
            pltpu.SemaphoreType.DMA((6,)),
            pltpu.SemaphoreType.DMA((wires,)),
            pltpu.SemaphoreType.DMA((wires,)),
            pltpu.SemaphoreType.DMA((NX * 2,)),
            pltpu.SemaphoreType.DMA((NZ,)),
        ],
        compiler_params=pltpu.CompilerParams(
            collective_id=0, has_side_effects=True, vmem_limit_bytes=63 << 20
        ),
        name="head_grad",
    )(
        hidden,
        head,
        gain.reshape(1, -1),
        refusal_ids.T,
        refusal_count.reshape(1, -1),
        loss_scale.reshape(1, -1),
    )
    return grad, log_refusal.reshape(-1)


def solution(mesh):
    return jax.shard_map(
        shards,
        mesh=mesh,
        in_specs=(
            P("prompt", None),
            P("prompt", "vocab"),
            P(),
            P("prompt", None),
            P("prompt"),
            P("prompt"),
        ),
        out_specs=(P("prompt", "vocab"), P("prompt")),
        check_vma=False,
    )
```

```python
import functools

import jax
import jax.numpy as jnp
from jax import lax
from jax.experimental import pallas as pl
from jax.experimental.pallas import tpu as pltpu
from jax.sharding import PartitionSpec as P

epsilon = 1e-05
lowest = -1e30
f32 = jnp.float32
bf16 = jnp.bfloat16

NX, NY, NZ, NC = 4, 4, 8, 2
R = 128
DL = 2048
VL = 1024
T = 256
KT = DL // T
VT = VL // T


class Wires:
    def __init__(self, send, recv):
        self.send, self.recv, self.used, self.open = send, recv, 0, []

    def describe(self, src, dst, device, index):
        return pltpu.make_async_remote_copy(
            src_ref=src,
            dst_ref=dst,
            send_sem=self.send.at[index],
            recv_sem=self.recv.at[index],
            device_id=device,
            device_id_type=pl.DeviceIdType.MESH,
        )

    def start(self, src, dst, device):
        copy = self.describe(src, dst, device, self.used)
        self.used += 1
        copy.start()
        self.open.append(copy)
        return copy

    def close(self):
        for copy in self.open:
            copy.wait_send()


def kernel(
    hid_hbm, head_hbm, gain_hbm, ids_hbm, count_hbm, loss_hbm, grad_ref, log_ref,
    hid, head, gain_ref, ids_ref, count_ref, loss_ref, inv_v, nfar, nsend, nrm, ptwo, pright, pleft, pown, hl, hr, inl, inr,
    mask, eall, eref, st1, st2, rs1, rs2, gt, gs, lent, own32,
    ytwo, yright, yleft, yhl, yhr, yinl, yinr, fsend, xrecv, frecv,
    load_sems, send_sems, recv_sems, fsend_sems, frecv_sems,
):
    p = lax.axis_index("prompt")
    v = lax.axis_index("vocab")
    c = v % NC
    y = (v // NC) % NY
    z = v // (NC * NY)

    def at(x_=p, y_=y, z_=z, c_=c):
        return (x_, (z_ * NY + y_) * NC + c_)

    def x_by(d):
        return at(x_=(p + d) % NX)

    def y_by(d):
        return at(y_=(y + d) % NY)

    def z_by(d):
        return at(z_=(z + d) % NZ)

    j_own = y * NC + c

    def plane_by(d):
        j = (j_own + d) % (NY * NC)
        return at(y_=j // NC, c_=j % NC), j

    sibling = at(c_=1 - c)

    load_hid = pltpu.make_async_copy(hid_hbm, hid, load_sems.at[0])
    load_gain = pltpu.make_async_copy(gain_hbm, gain_ref, load_sems.at[1])
    load_head = pltpu.make_async_copy(head_hbm, head, load_sems.at[2])
    load_ids = pltpu.make_async_copy(ids_hbm, ids_ref, load_sems.at[3])
    load_count = pltpu.make_async_copy(count_hbm, count_ref, load_sems.at[4])
    load_loss = pltpu.make_async_copy(loss_hbm, loss_ref, load_sems.at[5])
    loads = (load_hid, load_gain, load_head, load_ids, load_count, load_loss)
    for load in loads:
        load.start()

    barrier = pltpu.get_barrier_semaphore()

    def greet(device):
        pl.semaphore_signal(
            barrier, inc=1, device_id=device, device_id_type=pl.DeviceIdType.MESH
        )

    for d in range(1, NX):
        greet(x_by(d))
    for d in range(1, NY * NC):
        greet(plane_by(d)[0])
    for d in range(1, NZ):
        greet(z_by(d))
    corners = [(1, 1), (1, NZ - 1), (NY - 1, 1), (NY - 1, NZ - 1)]

    def corner(i):
        return at(y_=(y + corners[i][0]) % NY, z_=(z + corners[i][1]) % NZ)

    for i in range(4):
        greet(corner(i))

    wires = Wires(send_sems, recv_sems)

    lane = lax.broadcasted_iota(jnp.int32, (R, 128), 1)
    sub = lax.broadcasted_iota(jnp.int32, (R, 128), 0)

    def columns_of(rows):
        return jnp.concatenate([rows, jnp.zeros((R - 8, 128), f32)], axis=0).T

    load_hid.wait()

    def square(j, acc):
        x = hid[:, pl.ds(pl.multiple_of(j * 1024, 1024), 1024)].astype(f32)
        x = x * x
        for i in range(8):
            acc = acc + x[:, i * 128 : (i + 1) * 128]
        return acc

    acc = lax.fori_loop(0, 8, square, jnp.zeros((R, 128), f32))
    inv = lax.rsqrt(jnp.sum(acc, axis=1, keepdims=True) / 8192.0 + epsilon)
    inv_v[...] = jnp.broadcast_to(inv, (R, 128))
    load_gain.wait()

    def normed(col):
        col = pl.multiple_of(col, T)
        x = hid[:, pl.ds(col, T)].astype(f32)
        return (x * inv * gain_ref[:, pl.ds(col, T)]).astype(bf16)

    def piece_of(cc, dy, dz):
        return cc * 4 + (y + dy) % 2 * 2 + (z + dz) % 2

    nfar[...] = normed((p + 2) % NX * DL + piece_of(c, 0, 0) * T)

    pl.semaphore_wait(barrier, (NX - 1) + (NY * NC - 1) + (NZ - 1) + 4)

    up, down = y_by(1), y_by(NY - 1)
    right, left = x_by(1), x_by(NX - 1)
    half, other_half = pl.ds(c * NY, NY), pl.ds((1 - c) * NY, NY)
    own_piece = piece_of(c, 0, 0)
    come2 = wires.start(nfar, nrm.at[2, own_piece], x_by(2))
    come, shared = {}, {}
    for slot, i, device, d in ((3, 0, right, 1), (1, 1, left, NX - 1)):
        for k in range(NY):
            nsend[i, k] = normed((p + d) % NX * DL + (c * NY + k) * T)
        come[slot] = wires.start(nsend.at[i], nrm.at[slot, half], device)

    def rows_of(piece, i, n):
        return nrm.at[2, piece, pl.ds(i * (R // n), R // n)]

    sides = (up, down, z_by(1), z_by(NZ - 1))
    come2.wait_recv()
    spread_at = wires.used
    for i in range(4):
        part = rows_of(own_piece, i, 4)
        wires.start(part, part, corner(i))
    for i in range(4):
        part = rows_of(own_piece, i % 2, 2)
        wires.start(part, part, sides[i])

    def share_piece(dy, dz):
        whole = nrm.at[2, piece_of(c, dy, dz)]
        shared_at[dy, dz] = wires.used
        wires.start(whole, whole, sibling)

    shared_at = {}
    share_piece(0, 0)
    for k in range(KT):
        nrm[0, k] = normed(p * DL + k * T)
    for dy, dz, first in ((1, 0, 0), (0, 1, 2)):
        for i in range(2):
            part = rows_of(piece_of(c, dy, dz), i, 2)
            wires.describe(part, part, sides[first + i], spread_at + 4 + first + i).wait_recv()
        share_piece(dy, dz)
    for i in range(4):
        part = rows_of(piece_of(c, 1, 1), i, 4)
        wires.describe(part, part, corner(i), spread_at + i).wait_recv()
    share_piece(1, 1)

    def share(slot):
        come[slot].wait_recv()
        rows = nrm.at[slot, half]
        shared[slot, "at"] = wires.used
        wires.start(rows, rows, sibling)

    def wait_share(slot):
        if slot == 2:
            for (dy, dz), index in shared_at.items():
                rows = nrm.at[2, piece_of(1 - c, dy, dz)]
                wires.describe(rows, rows, sibling, index).wait_recv()
        else:
            rows = nrm.at[slot, other_half]
            wires.describe(rows, rows, sibling, shared[slot, "at"]).wait_recv()

    def partial(s, t):
        lhs = jnp.concatenate([nrm[s, k] for k in range(KT)], axis=1)
        return jnp.dot(lhs, head[:, t * T : (t + 1) * T], preferred_element_type=f32)

    load_head.wait()
    wait_share(2)
    ch_l, ch_r, cin_l, cin_r = {}, {}, {}, {}
    for t in (0, 2, 1, 3):
        ptwo[t] = partial(2, t)
        if t < 2:
            ch_l[t] = wires.start(ptwo.at[t], hl.at[t], right)
        else:
            ch_r[t - 2] = wires.start(ptwo.at[t], hr.at[t - 2], left)
    share(3)
    share(1)
    wait_share(1)
    for t in (2, 3):
        pright[t] = partial(1, t)
        cin_l[t] = wires.start(pright.at[t], inl.at[t], right)
    wait_share(3)
    for t in (0, 1):
        pleft[t] = partial(3, t)
        cin_r[t] = wires.start(pleft.at[t], inr.at[t], left)
    for t in (0, 1):
        pright[t] = partial(1, t)
        pleft[t + 2] = partial(3, t + 2)
    for t in (0, 1):
        ch_l[t].wait_recv()
        pright[t] = pright[t] + hl[t]
        cin_l[t] = wires.start(pright.at[t], inl.at[t], right)
        ch_r[t].wait_recv()
        pleft[t + 2] = pleft[t + 2] + hr[t]
        cin_r[t + 2] = wires.start(pleft.at[t + 2], inr.at[t + 2], left)
    lend = {}
    for b in range(2 * NY):
        rows = pl.ds(pl.multiple_of((b * NC + 1 - c) * 128, 128), 128)
        lend[b] = wires.start(head.at[rows], lent.at[b], sibling)
    for t in range(VT):
        pown[t] = partial(0, t)

    load_ids.wait()
    load_count.wait()
    load_loss.wait()
    ids = jnp.concatenate([ids_ref[...], jnp.zeros((R - 16, 128), jnp.int32)], axis=0).T
    cl = jnp.where(
        sub == 0,
        jnp.broadcast_to(count_ref[...].astype(f32), (R, 128)),
        jnp.where(sub == 1, jnp.broadcast_to(loss_ref[...], (R, 128)), 0.0),
    ).T
    count_col, loss_col = cl[:, 0:1], cl[:, 1:2]
    wide = lax.broadcasted_iota(jnp.int32, (R, T), 1)
    for t in range(VT):
        hit = jnp.zeros((R, T), jnp.int32)
        for k in range(16):
            here = ids[:, k : k + 1] - (v * VL + t * T)
            here = jnp.where(count_col > float(k), here, -1)
            hit = jnp.where(wide == here, 1, hit)
        mask[t] = hit

    m_all = jnp.full((R, T), -3e38, f32)
    m_ref = jnp.full((R, T), lowest, f32)
    for t in (2, 3, 0, 1):
        cin_l[t].wait_recv()
        cin_r[t].wait_recv()
        logit = pown[t] + inl[t] + inr[t]
        pown[t] = logit
        m_all = jnp.maximum(m_all, logit)
        m_ref = jnp.maximum(m_ref, jnp.where(mask[t] > 0, logit, lowest))
    m_all = jnp.max(m_all, axis=1, keepdims=True)
    m_ref = jnp.max(m_ref, axis=1, keepdims=True)
    s_all = jnp.zeros((R, T), f32)
    s_ref = jnp.zeros((R, T), f32)
    for t in range(VT):
        logit = pown[t]
        e = jnp.exp(logit - m_all)
        r = jnp.exp(jnp.where(mask[t] > 0, logit - m_ref, lowest))
        eall[t] = e
        eref[t] = r
        s_all = s_all + e
        s_ref = s_ref + r
    s_all = jnp.sum(s_all, axis=1, keepdims=True)
    s_ref = jnp.sum(s_ref, axis=1, keepdims=True)

    packed = jnp.where(lane == 0, m_all, jnp.zeros((R, 128), f32))
    packed = jnp.where(lane == 1, m_ref, packed)
    packed = jnp.where(lane == 8, s_all, packed)
    packed = jnp.where(lane == 9, s_ref, packed)
    packed = packed.T
    st1[j_own, 0] = packed[0:8]
    st1[j_own, 1] = packed[8:16]

    def spread_plane(buf):
        first = wires.used
        for d in range(1, NY * NC):
            wires.start(buf.at[j_own], buf.at[j_own], plane_by(d)[0])
        return first

    def await_plane(buf, first):
        for d in range(1, NY * NC):
            device, j = plane_by(NY * NC - d)
            wires.describe(buf.at[j], buf.at[j], device, first + d - 1).wait_recv()

    def spread_line(buf):
        first = wires.used
        for d in range(1, NZ):
            wires.start(buf.at[z], buf.at[z], z_by(d))
        return first

    def await_line(buf, first):
        for d in range(1, NZ):
            zz = (z + NZ - d) % NZ
            wires.describe(buf.at[zz], buf.at[zz], at(z_=zz), first + d - 1).wait_recv()

    def merged(buf, n):
        peak = buf[0, 0]
        for j in range(1, n):
            peak = jnp.maximum(peak, buf[j, 0])
        total = buf[0, 1] * jnp.exp(buf[0, 0] - peak)
        for j in range(1, n):
            total = total + buf[j, 1] * jnp.exp(buf[j, 0] - peak)
        return peak, total

    first = spread_plane(st1)
    await_plane(st1, first)
    peak, total = merged(st1, NY * NC)
    st2[z, 0] = peak
    st2[z, 1] = total
    first = spread_line(st2)
    await_line(st2, first)
    peak, total = merged(st2, NZ)
    row8 = lax.broadcasted_iota(jnp.int32, (8, 128), 0)
    lse = peak + jnp.log(jnp.where(row8 < 2, total, 1.0))
    log_ref[...] = lse[1:2] - lse[0:1]
    lse_cols = columns_of(lse)
    f_all = loss_col * jnp.exp(m_all - lse_cols[:, 0:1])
    f_ref = loss_col * jnp.exp(m_ref - lse_cols[:, 1:2])

    rt = jnp.zeros((R, T), f32)
    to_right, to_left = {}, {}
    def gather(t_r, t_l):
        to_right[t_r] = wires.start(gt.at[0, t_r], gt.at[3, t_r], right)
        to_left[t_l] = wires.start(gt.at[0, t_l], gt.at[1, t_l], left)

    for pair in ((0, 2), (1, 3)):
        for t in pair:
            g = eref[t] * f_ref - eall[t] * f_all
            g = g.astype(bf16)
            gt[0, t] = g
            rt = rt + g.astype(f32) * pown[t]
        gather(*pair)
    gather(2, 0)
    gather(3, 1)
    lot = {}

    def to_sibling(s, t):
        lot[s, t] = wires.start(gt.at[s, t], gs.at[s, t], sibling)

    for t in (0, 2, 1, 3):
        to_sibling(0, t)
    rt = jnp.sum(rt, axis=1, keepdims=True)
    rs1[j_own] = jnp.where(lane == 0, rt, jnp.zeros((R, 128), f32)).T[0:8]
    rt_first = spread_plane(rs1)

    yl2, yr2, yl, yr = {}, {}, {}, {}
    y1, y2, y3 = ((y + d) % NY for d in (1, 2, 3))

    def multiply(s):
        def times(block, tiles):
            rhs = jnp.concatenate([tiles[s, t] for t in range(VT)], axis=1).T
            return jnp.dot(block, rhs, preferred_element_type=f32).reshape(NY, 128, R)

        for zl in range(2):
            rows = [
                pl.multiple_of(((zl * NY + yy) * NC + c) * 128, 128)
                for yy in range(NY)
            ]
            here = jnp.concatenate([head[pl.ds(row, 128), :] for row in rows], axis=0)
            own32[s, zl] = times(here, gt)
        for t in range(VT):
            lot[s, t].wait_recv()
        for zl in range(2):
            block = lent[zl * NY : (zl + 1) * NY].reshape(NY * 128, VL)
            own32[s, zl] = own32[s, zl] + times(block, gs)
            y_first(s, zl)

    def y_first(s, zl):
        ytwo[s, zl] = own32[s, zl, y2].astype(bf16)
        if zl == 0:
            yl2[s] = wires.start(ytwo.at[s, 0], yhl.at[s], up)
            yleft[s, 0] = own32[s, 0, y3].astype(bf16)
            yr[s, 0] = wires.start(yleft.at[s, 0], yinr.at[s, 0], down)
        else:
            yr2[s] = wires.start(ytwo.at[s, 1], yhr.at[s], down)
            yright[s, 1] = own32[s, 1, y1].astype(bf16)
            yl[s, 1] = wires.start(yright.at[s, 1], yinl.at[s, 1], up)

    def y_second(s):
        yl2[s].wait_recv()
        yright[s, 0] = (own32[s, 0, y1] + yhl[s].astype(f32)).astype(bf16)
        yl[s, 0] = wires.start(yright.at[s, 0], yinl.at[s, 0], up)
        yr2[s].wait_recv()
        yleft[s, 1] = (own32[s, 1, y3] + yhr[s].astype(f32)).astype(bf16)
        yr[s, 1] = wires.start(yleft.at[s, 1], yinr.at[s, 1], down)

    def place(s, zl):
        return pltpu.make_async_remote_copy(
            src_ref=xrecv.at[s, zl],
            dst_ref=frecv.at[z],
            send_sem=fsend_sems.at[s * 2 + zl],
            recv_sem=frecv_sems.at[z],
            device_id=at(z_=(p + NX - s) % NX * 2 + zl),
            device_id_type=pl.DeviceIdType.MESH,
        )

    move = {}

    def y_third(s):
        for zl in (1, 0):
            yl[s, zl].wait_recv()
            yr[s, zl].wait_recv()
            out = own32[s, zl, y]
            out = out + yinl[s, zl].astype(f32) + yinr[s, zl].astype(f32)
            if s:
                fsend[s, zl] = out.astype(bf16)
                move[s, zl] = wires.start(fsend.at[s, zl], xrecv.at[s, zl], x_by(s))
            else:
                xrecv[s, zl] = out.astype(bf16)

    def z_out(s):
        for zl in (1, 0):
            if s:
                move[s, zl].wait_recv()
            there_z = (p + NX - s) % NX * 2 + zl

            @pl.when(z != there_z)
            def _():
                place(s, zl).start()

            @pl.when(z == there_z)
            def _():
                frecv[z] = xrecv[s, zl]

    for b in range(2 * NY):
        lend[b].wait_recv()
    multiply(0)
    for t in (0, 1):
        to_right[t].wait_recv()
        wires.start(gt.at[3, t], gt.at[2, t], right)
        to_left[t + 2].wait_recv()
        wires.start(gt.at[1, t + 2], gt.at[2, t + 2], left)
        to_sibling(3, t)
        to_sibling(1, t + 2)
    forward = wires.used - 8
    for t in (2, 3):
        to_right[t].wait_recv()
        to_sibling(3, t)
        to_left[t - 2].wait_recv()
        to_sibling(1, t - 2)
    y_second(0)
    multiply(3)
    multiply(1)
    y_third(0)
    z_out(0)
    for t in (0, 1):
        for i, tile, device in ((0, t, left), (1, t + 2, right)):
            wires.describe(
                gt.at[2, tile], gt.at[2, tile], device, forward + 4 * t + i
            ).wait_recv()
            to_sibling(2, tile)
    multiply(2)
    await_plane(rs1, rt_first)
    total = rs1[0]
    for j in range(1, NY * NC):
        total = total + rs1[j]
    rs2[z] = total
    rt_first = spread_line(rs2)
    y_second(3)
    y_second(1)
    y_second(2)
    y_third(3)
    y_third(1)
    y_third(2)
    z_out(3)
    z_out(1)
    await_line(rs2, rt_first)
    total = rs2[0]
    for j in range(1, NZ):
        total = total + rs2[j]
    rt_col = columns_of(total)[:, 0:1]
    z_out(2)

    own_cols = pl.ds(pl.multiple_of(v * 128, 128), 128)
    inv = inv_v[...]
    minus = hid[:, own_cols].astype(f32) * (inv * inv / 8192.0) * rt_col
    scale = inv * gain_ref[:, own_cols]
    for zs in range(NZ):

        @pl.when(zs != z)
        def _():
            pltpu.make_async_remote_copy(
                src_ref=frecv.at[zs],
                dst_ref=frecv.at[zs],
                send_sem=fsend_sems.at[0],
                recv_sem=frecv_sems.at[zs],
                device_id=at(z_=zs),
                device_id_type=pl.DeviceIdType.MESH,
            ).wait_recv()

    total = frecv[0].astype(f32)
    for zs in range(1, NZ):
        total = total + frecv[zs].astype(f32)
    grad_ref[...] = scale * total.T - minus

    wires.close()
    for s in range(NX):
        for zl in range(2):

            @pl.when(z != (p + NX - s) % NX * 2 + zl)
            def _():
                place(s, zl).wait_send()


def shards(hidden, head, gain, refusal_ids, refusal_count, loss_scale):
    V = pltpu.VMEM
    tile = (R, T)
    box = (R, 128)
    wires = 140
    grad, log_refusal = pl.pallas_call(
        kernel,
        out_shape=(
            jax.ShapeDtypeStruct((R, 128), f32),
            jax.ShapeDtypeStruct((1, R), f32),
        ),
        in_specs=[pl.BlockSpec(memory_space=pltpu.HBM)] * 6,
        out_specs=(pl.BlockSpec(memory_space=pltpu.VMEM),) * 2,
        scratch_shapes=[
            V((R, NX * DL), bf16),
            V((DL, VL), bf16),
            V((1, NX * DL), f32),
            V((16, R), jnp.int32),
            V((1, R), jnp.int32),
            V((1, R), f32),
            V(box, f32),
            V(tile, bf16),
            V((2, NY) + tile, bf16),
            V((NX, KT) + tile, bf16),
            V((VT,) + tile, f32),
            V((VT,) + tile, f32),
            V((VT,) + tile, f32),
            V((VT,) + tile, f32),
            V((2,) + tile, f32),
            V((2,) + tile, f32),
            V((VT,) + tile, f32),
            V((VT,) + tile, f32),
            V((VT,) + tile, jnp.int32),
            V((VT,) + tile, f32),
            V((VT,) + tile, f32),
            V((NY * NC, 2, 8, 128), f32),
            V((NZ, 2, 8, 128), f32),
            V((NY * NC, 8, 128), f32),
            V((NZ, 8, 128), f32),
            V((NX, VT) + tile, bf16),
            V((NX, VT) + tile, bf16),
            V((2 * NY, 128, VL), bf16),
            V((NX, 2, NY) + box, f32),
            V((NX, 2) + box, bf16),
            V((NX, 2) + box, bf16),
            V((NX, 2) + box, bf16),
            V((NX,) + box, bf16),
            V((NX,) + box, bf16),
            V((NX, 2) + box, bf16),
            V((NX, 2) + box, bf16),
            V((NX, 2) + box, bf16),
            V((NX, 2) + box, bf16),
            V((NZ,) + box, bf16),
            pltpu.SemaphoreType.DMA((6,)),
            pltpu.SemaphoreType.DMA((wires,)),
            pltpu.SemaphoreType.DMA((wires,)),
            pltpu.SemaphoreType.DMA((NX * 2,)),
            pltpu.SemaphoreType.DMA((NZ,)),
        ],
        compiler_params=pltpu.CompilerParams(
            collective_id=0, has_side_effects=True, vmem_limit_bytes=63 << 20
        ),
        name="head_grad",
    )(
        hidden,
        head,
        gain.reshape(1, -1),
        refusal_ids.T,
        refusal_count.reshape(1, -1),
        loss_scale.reshape(1, -1),
    )
    return grad, log_refusal.reshape(-1)


def solution(mesh):
    return jax.shard_map(
        shards,
        mesh=mesh,
        in_specs=(
            P("prompt", None),
            P("prompt", "vocab"),
            P(),
            P("prompt", None),
            P("prompt"),
            P("prompt"),
        ),
        out_specs=(P("prompt", "vocab"), P("prompt")),
        check_vma=False,
    )
```

```python
import functools

import jax
import jax.numpy as jnp
from jax import lax
from jax.experimental import pallas as pl
from jax.experimental.pallas import tpu as pltpu
from jax.sharding import PartitionSpec as P

epsilon = 1e-05
lowest = -1e30
f32 = jnp.float32
bf16 = jnp.bfloat16

NX, NY, NZ, NC = 4, 4, 8, 2
R = 128
DL = 2048
VL = 1024
T = 256
KT = DL // T
VT = VL // T


class Wires:
    def __init__(self, send, recv):
        self.send, self.recv, self.used, self.open = send, recv, 0, []

    def describe(self, src, dst, device, index):
        return pltpu.make_async_remote_copy(
            src_ref=src,
            dst_ref=dst,
            send_sem=self.send.at[index],
            recv_sem=self.recv.at[index],
            device_id=device,
            device_id_type=pl.DeviceIdType.MESH,
        )

    def start(self, src, dst, device):
        copy = self.describe(src, dst, device, self.used)
        self.used += 1
        copy.start()
        self.open.append(copy)
        return copy

    def close(self):
        for copy in self.open:
            copy.wait_send()


def kernel(
    hid_hbm, head_hbm, gain_hbm, ids_hbm, count_hbm, loss_hbm, grad_ref, log_ref,
    hid, head, gain_ref, ids_ref, count_ref, loss_ref, inv_v, nfar, nsend, nrm, ptwo, pright, pleft, pown, hl, hr, inl, inr,
    mask, eall, eref, st1, st2, rs1, rs2, gt, gs, lent, own32,
    ytwo, yright, yleft, yhl, yhr, yinl, yinr, fsend, xrecv, frecv,
    load_sems, send_sems, recv_sems, fsend_sems, frecv_sems,
):
    p = lax.axis_index("prompt")
    v = lax.axis_index("vocab")
    c = v % NC
    y = (v // NC) % NY
    z = v // (NC * NY)

    def at(x_=p, y_=y, z_=z, c_=c):
        return (x_, (z_ * NY + y_) * NC + c_)

    def x_by(d):
        return at(x_=(p + d) % NX)

    def y_by(d):
        return at(y_=(y + d) % NY)

    def z_by(d):
        return at(z_=(z + d) % NZ)

    j_own = y * NC + c

    def plane_by(d):
        j = (j_own + d) % (NY * NC)
        return at(y_=j // NC, c_=j % NC), j

    sibling = at(c_=1 - c)

    load_hid = pltpu.make_async_copy(hid_hbm, hid, load_sems.at[0])
    load_gain = pltpu.make_async_copy(gain_hbm, gain_ref, load_sems.at[1])
    load_head = pltpu.make_async_copy(head_hbm, head, load_sems.at[2])
    load_ids = pltpu.make_async_copy(ids_hbm, ids_ref, load_sems.at[3])
    load_count = pltpu.make_async_copy(count_hbm, count_ref, load_sems.at[4])
    load_loss = pltpu.make_async_copy(loss_hbm, loss_ref, load_sems.at[5])
    loads = (load_hid, load_gain, load_head, load_ids, load_count, load_loss)
    for load in loads:
        load.start()

    barrier = pltpu.get_barrier_semaphore()

    def greet(device):
        pl.semaphore_signal(
            barrier, inc=1, device_id=device, device_id_type=pl.DeviceIdType.MESH
        )

    for d in range(1, NX):
        greet(x_by(d))
    for d in range(1, NY * NC):
        greet(plane_by(d)[0])
    for d in range(1, NZ):
        greet(z_by(d))
    corners = [(1, 1), (1, NZ - 1), (NY - 1, 1), (NY - 1, NZ - 1)]

    def corner(i):
        return at(y_=(y + corners[i][0]) % NY, z_=(z + corners[i][1]) % NZ)

    for i in range(4):
        greet(corner(i))

    wires = Wires(send_sems, recv_sems)

    lane = lax.broadcasted_iota(jnp.int32, (R, 128), 1)
    sub = lax.broadcasted_iota(jnp.int32, (R, 128), 0)

    def columns_of(rows):
        return jnp.concatenate([rows, jnp.zeros((R - 8, 128), f32)], axis=0).T

    load_hid.wait()

    def square(j, acc):
        x = hid[:, pl.ds(pl.multiple_of(j * 1024, 1024), 1024)].astype(f32)
        x = x * x
        for i in range(8):
            acc = acc + x[:, i * 128 : (i + 1) * 128]
        return acc

    acc = lax.fori_loop(0, 8, square, jnp.zeros((R, 128), f32))
    inv = lax.rsqrt(jnp.sum(acc, axis=1, keepdims=True) / 8192.0 + epsilon)
    inv_v[...] = jnp.broadcast_to(inv, (R, 128))
    load_gain.wait()

    def normed(col):
        col = pl.multiple_of(col, T)
        x = hid[:, pl.ds(col, T)].astype(f32)
        return (x * inv * gain_ref[:, pl.ds(col, T)]).astype(bf16)

    def piece_of(cc, dy, dz):
        return cc * 4 + (y + dy) % 2 * 2 + (z + dz) % 2

    nfar[...] = normed((p + 2) % NX * DL + piece_of(c, 0, 0) * T)

    pl.semaphore_wait(barrier, (NX - 1) + (NY * NC - 1) + (NZ - 1) + 4)

    up, down = y_by(1), y_by(NY - 1)
    right, left = x_by(1), x_by(NX - 1)
    half, other_half = pl.ds(c * NY, NY), pl.ds((1 - c) * NY, NY)
    own_piece = piece_of(c, 0, 0)
    come2 = wires.start(nfar, nrm.at[2, own_piece], x_by(2))
    come, shared = {}, {}
    for i, d in ((0, 1), (1, NX - 1)):
        for k in range(NY):
            nsend[i, k] = normed((p + d) % NX * DL + (c * NY + k) * T)

    def rows_of(piece, i, n):
        return nrm.at[2, piece, pl.ds(i * (R // n), R // n)]

    sides = (up, down, z_by(1), z_by(NZ - 1))
    come2.wait_recv()
    spread_at = wires.used
    for i in range(4):
        part = rows_of(own_piece, i, 4)
        wires.start(part, part, corner(i))
    for i in range(4):
        part = rows_of(own_piece, i % 2, 2)
        wires.start(part, part, sides[i])

    come[3] = wires.start(nsend.at[0], nrm.at[3, half], right)
    come[1] = wires.start(nsend.at[1], nrm.at[1, half], left)

    def share_piece(dy, dz):
        whole = nrm.at[2, piece_of(c, dy, dz)]
        shared_at[dy, dz] = wires.used
        wires.start(whole, whole, sibling)

    shared_at = {}
    share_piece(0, 0)
    for k in range(KT):
        nrm[0, k] = normed(p * DL + k * T)
    for dy, dz, first in ((1, 0, 0), (0, 1, 2)):
        for i in range(2):
            part = rows_of(piece_of(c, dy, dz), i, 2)
            wires.describe(part, part, sides[first + i], spread_at + 4 + first + i).wait_recv()
        share_piece(dy, dz)
    for i in range(4):
        part = rows_of(piece_of(c, 1, 1), i, 4)
        wires.describe(part, part, corner(i), spread_at + i).wait_recv()
    share_piece(1, 1)

    def share(slot):
        come[slot].wait_recv()
        rows = nrm.at[slot, half]
        shared[slot, "at"] = wires.used
        wires.start(rows, rows, sibling)

    def wait_share(slot):
        if slot == 2:
            for (dy, dz), index in shared_at.items():
                rows = nrm.at[2, piece_of(1 - c, dy, dz)]
                wires.describe(rows, rows, sibling, index).wait_recv()
        else:
            rows = nrm.at[slot, other_half]
            wires.describe(rows, rows, sibling, shared[slot, "at"]).wait_recv()

    def partial(s, t):
        lhs = jnp.concatenate([nrm[s, k] for k in range(KT)], axis=1)
        return jnp.dot(lhs, head[:, t * T : (t + 1) * T], preferred_element_type=f32)

    load_head.wait()
    wait_share(2)
    ch_l, ch_r, cin_l, cin_r = {}, {}, {}, {}
    for t in (0, 2, 1, 3):
        ptwo[t] = partial(2, t)
        if t < 2:
            ch_l[t] = wires.start(ptwo.at[t], hl.at[t], right)
        else:
            ch_r[t - 2] = wires.start(ptwo.at[t], hr.at[t - 2], left)
    share(3)
    share(1)
    wait_share(1)
    for t in (2, 3):
        pright[t] = partial(1, t)
        cin_l[t] = wires.start(pright.at[t], inl.at[t], right)
    wait_share(3)
    for t in (0, 1):
        pleft[t] = partial(3, t)
        cin_r[t] = wires.start(pleft.at[t], inr.at[t], left)
    for t in (0, 1):
        pright[t] = partial(1, t)
        pleft[t + 2] = partial(3, t + 2)
    for t in (0, 1):
        ch_l[t].wait_recv()
        pright[t] = pright[t] + hl[t]
        cin_l[t] = wires.start(pright.at[t], inl.at[t], right)
        ch_r[t].wait_recv()
        pleft[t + 2] = pleft[t + 2] + hr[t]
        cin_r[t + 2] = wires.start(pleft.at[t + 2], inr.at[t + 2], left)
    lend = {}
    for b in range(2 * NY):
        rows = pl.ds(pl.multiple_of((b * NC + 1 - c) * 128, 128), 128)
        lend[b] = wires.start(head.at[rows], lent.at[b], sibling)
    for t in range(VT):
        pown[t] = partial(0, t)

    load_ids.wait()
    load_count.wait()
    load_loss.wait()
    ids = jnp.concatenate([ids_ref[...], jnp.zeros((R - 16, 128), jnp.int32)], axis=0).T
    cl = jnp.where(
        sub == 0,
        jnp.broadcast_to(count_ref[...].astype(f32), (R, 128)),
        jnp.where(sub == 1, jnp.broadcast_to(loss_ref[...], (R, 128)), 0.0),
    ).T
    count_col, loss_col = cl[:, 0:1], cl[:, 1:2]
    wide = lax.broadcasted_iota(jnp.int32, (R, T), 1)
    for t in range(VT):
        hit = jnp.zeros((R, T), jnp.int32)
        for k in range(16):
            here = ids[:, k : k + 1] - (v * VL + t * T)
            here = jnp.where(count_col > float(k), here, -1)
            hit = jnp.where(wide == here, 1, hit)
        mask[t] = hit

    m_all = jnp.full((R, T), -3e38, f32)
    m_ref = jnp.full((R, T), lowest, f32)
    for t in (2, 3, 0, 1):
        cin_l[t].wait_recv()
        cin_r[t].wait_recv()
        logit = pown[t] + inl[t] + inr[t]
        pown[t] = logit
        m_all = jnp.maximum(m_all, logit)
        m_ref = jnp.maximum(m_ref, jnp.where(mask[t] > 0, logit, lowest))
    m_all = jnp.max(m_all, axis=1, keepdims=True)
    m_ref = jnp.max(m_ref, axis=1, keepdims=True)
    s_all = jnp.zeros((R, T), f32)
    s_ref = jnp.zeros((R, T), f32)
    for t in range(VT):
        logit = pown[t]
        e = jnp.exp(logit - m_all)
        r = jnp.exp(jnp.where(mask[t] > 0, logit - m_ref, lowest))
        eall[t] = e
        eref[t] = r
        s_all = s_all + e
        s_ref = s_ref + r
    s_all = jnp.sum(s_all, axis=1, keepdims=True)
    s_ref = jnp.sum(s_ref, axis=1, keepdims=True)

    packed = jnp.where(lane == 0, m_all, jnp.zeros((R, 128), f32))
    packed = jnp.where(lane == 1, m_ref, packed)
    packed = jnp.where(lane == 8, s_all, packed)
    packed = jnp.where(lane == 9, s_ref, packed)
    packed = packed.T
    st1[j_own, 0] = packed[0:8]
    st1[j_own, 1] = packed[8:16]

    far_first = (4, 3, 5, 2, 6, 1, 7)

    def spread_plane(buf):
        first = wires.used
        for d in far_first:
            wires.start(buf.at[j_own], buf.at[j_own], plane_by(d)[0])
        return first

    def await_plane(buf, first):
        for i, d in enumerate(far_first):
            device, j = plane_by(NY * NC - d)
            wires.describe(buf.at[j], buf.at[j], device, first + i).wait_recv()

    def spread_line(buf):
        first = wires.used
        for d in far_first:
            wires.start(buf.at[z], buf.at[z], z_by(d))
        return first

    def await_line(buf, first):
        for i, d in enumerate(far_first):
            zz = (z + NZ - d) % NZ
            wires.describe(buf.at[zz], buf.at[zz], at(z_=zz), first + i).wait_recv()

    def merged(buf, n):
        peak = buf[0, 0]
        for j in range(1, n):
            peak = jnp.maximum(peak, buf[j, 0])
        total = buf[0, 1] * jnp.exp(buf[0, 0] - peak)
        for j in range(1, n):
            total = total + buf[j, 1] * jnp.exp(buf[j, 0] - peak)
        return peak, total

    first = spread_plane(st1)
    await_plane(st1, first)
    peak, total = merged(st1, NY * NC)
    st2[z, 0] = peak
    st2[z, 1] = total
    first = spread_line(st2)
    await_line(st2, first)
    peak, total = merged(st2, NZ)
    row8 = lax.broadcasted_iota(jnp.int32, (8, 128), 0)
    lse = peak + jnp.log(jnp.where(row8 < 2, total, 1.0))
    log_ref[...] = lse[1:2] - lse[0:1]
    lse_cols = columns_of(lse)
    f_all = loss_col * jnp.exp(m_all - lse_cols[:, 0:1])
    f_ref = loss_col * jnp.exp(m_ref - lse_cols[:, 1:2])

    rt = jnp.zeros((R, T), f32)
    to_right, to_left = {}, {}
    def gather(t_r, t_l):
        to_right[t_r] = wires.start(gt.at[0, t_r], gt.at[3, t_r], right)
        to_left[t_l] = wires.start(gt.at[0, t_l], gt.at[1, t_l], left)

    for pair in ((0, 2), (1, 3)):
        for t in pair:
            g = eref[t] * f_ref - eall[t] * f_all
            g = g.astype(bf16)
            gt[0, t] = g
            rt = rt + g.astype(f32) * pown[t]
        gather(*pair)
    gather(2, 0)
    gather(3, 1)
    lot = {}

    def to_sibling(s, t):
        lot[s, t] = wires.start(gt.at[s, t], gs.at[s, t], sibling)

    for t in (0, 2, 1, 3):
        to_sibling(0, t)
    rt = jnp.sum(rt, axis=1, keepdims=True)
    rs1[j_own] = jnp.where(lane == 0, rt, jnp.zeros((R, 128), f32)).T[0:8]
    rt_first = spread_plane(rs1)

    yl2, yr2, yl, yr = {}, {}, {}, {}
    y1, y2, y3 = ((y + d) % NY for d in (1, 2, 3))

    def multiply(s):
        def times(block, tiles):
            rhs = jnp.concatenate([tiles[s, t] for t in range(VT)], axis=1).T
            return jnp.dot(block, rhs, preferred_element_type=f32).reshape(NY, 128, R)

        for zl in range(2):
            rows = [
                pl.multiple_of(((zl * NY + yy) * NC + c) * 128, 128)
                for yy in range(NY)
            ]
            here = jnp.concatenate([head[pl.ds(row, 128), :] for row in rows], axis=0)
            own32[s, zl] = times(here, gt)
        for t in range(VT):
            lot[s, t].wait_recv()
        for zl in range(2):
            block = lent[zl * NY : (zl + 1) * NY].reshape(NY * 128, VL)
            own32[s, zl] = own32[s, zl] + times(block, gs)
            y_first(s, zl)

    def y_first(s, zl):
        ytwo[s, zl] = own32[s, zl, y2].astype(bf16)
        if zl == 0:
            yl2[s] = wires.start(ytwo.at[s, 0], yhl.at[s], up)
            yleft[s, 0] = own32[s, 0, y3].astype(bf16)
            yr[s, 0] = wires.start(yleft.at[s, 0], yinr.at[s, 0], down)
        else:
            yr2[s] = wires.start(ytwo.at[s, 1], yhr.at[s], down)
            yright[s, 1] = own32[s, 1, y1].astype(bf16)
            yl[s, 1] = wires.start(yright.at[s, 1], yinl.at[s, 1], up)

    def y_second(s):
        yl2[s].wait_recv()
        yright[s, 0] = (own32[s, 0, y1] + yhl[s].astype(f32)).astype(bf16)
        yl[s, 0] = wires.start(yright.at[s, 0], yinl.at[s, 0], up)
        yr2[s].wait_recv()
        yleft[s, 1] = (own32[s, 1, y3] + yhr[s].astype(f32)).astype(bf16)
        yr[s, 1] = wires.start(yleft.at[s, 1], yinr.at[s, 1], down)

    def place(s, zl):
        return pltpu.make_async_remote_copy(
            src_ref=xrecv.at[s, zl],
            dst_ref=frecv.at[z],
            send_sem=fsend_sems.at[s * 2 + zl],
            recv_sem=frecv_sems.at[z],
            device_id=at(z_=(p + NX - s) % NX * 2 + zl),
            device_id_type=pl.DeviceIdType.MESH,
        )

    move = {}

    def y_third(s):
        for zl in (1, 0):
            yl[s, zl].wait_recv()
            yr[s, zl].wait_recv()
            out = own32[s, zl, y]
            out = out + yinl[s, zl].astype(f32) + yinr[s, zl].astype(f32)
            if s:
                fsend[s, zl] = out.astype(bf16)
                move[s, zl] = wires.start(fsend.at[s, zl], xrecv.at[s, zl], x_by(s))
            else:
                xrecv[s, zl] = out.astype(bf16)

    def z_out(s):
        for zl in (1, 0):
            if s:
                move[s, zl].wait_recv()
            there_z = (p + NX - s) % NX * 2 + zl

            @pl.when(z != there_z)
            def _():
                place(s, zl).start()

            @pl.when(z == there_z)
            def _():
                frecv[z] = xrecv[s, zl]

    for b in range(2 * NY):
        lend[b].wait_recv()
    multiply(0)
    for t in (0, 1):
        to_right[t].wait_recv()
        wires.start(gt.at[3, t], gt.at[2, t], right)
        to_left[t + 2].wait_recv()
        wires.start(gt.at[1, t + 2], gt.at[2, t + 2], left)
        to_sibling(3, t)
        to_sibling(1, t + 2)
    forward = wires.used - 8
    for t in (2, 3):
        to_right[t].wait_recv()
        to_sibling(3, t)
        to_left[t - 2].wait_recv()
        to_sibling(1, t - 2)
    y_second(0)
    multiply(3)
    multiply(1)
    y_third(0)
    z_out(0)
    await_plane(rs1, rt_first)
    total = rs1[0]
    for j in range(1, NY * NC):
        total = total + rs1[j]
    rs2[z] = total
    rt_first = spread_line(rs2)
    for t in (0, 1):
        for i, tile, device in ((0, t, left), (1, t + 2, right)):
            wires.describe(
                gt.at[2, tile], gt.at[2, tile], device, forward + 4 * t + i
            ).wait_recv()
            to_sibling(2, tile)
    multiply(2)
    y_second(3)
    y_second(1)
    y_second(2)
    y_third(3)
    y_third(1)
    y_third(2)
    z_out(3)
    z_out(1)
    await_line(rs2, rt_first)
    total = rs2[0]
    for j in range(1, NZ):
        total = total + rs2[j]
    rt_col = columns_of(total)[:, 0:1]
    z_out(2)

    own_cols = pl.ds(pl.multiple_of(v * 128, 128), 128)
    inv = inv_v[...]
    minus = hid[:, own_cols].astype(f32) * (inv * inv / 8192.0) * rt_col
    scale = inv * gain_ref[:, own_cols]
    for zs in range(NZ):

        @pl.when(zs != z)
        def _():
            pltpu.make_async_remote_copy(
                src_ref=frecv.at[zs],
                dst_ref=frecv.at[zs],
                send_sem=fsend_sems.at[0],
                recv_sem=frecv_sems.at[zs],
                device_id=at(z_=zs),
                device_id_type=pl.DeviceIdType.MESH,
            ).wait_recv()

    total = frecv[0].astype(f32)
    for zs in range(1, NZ):
        total = total + frecv[zs].astype(f32)
    grad_ref[...] = scale * total.T - minus

    wires.close()
    for s in range(NX):
        for zl in range(2):

            @pl.when(z != (p + NX - s) % NX * 2 + zl)
            def _():
                place(s, zl).wait_send()


def shards(hidden, head, gain, refusal_ids, refusal_count, loss_scale):
    V = pltpu.VMEM
    tile = (R, T)
    box = (R, 128)
    wires = 140
    grad, log_refusal = pl.pallas_call(
        kernel,
        out_shape=(
            jax.ShapeDtypeStruct((R, 128), f32),
            jax.ShapeDtypeStruct((1, R), f32),
        ),
        in_specs=[pl.BlockSpec(memory_space=pltpu.HBM)] * 6,
        out_specs=(pl.BlockSpec(memory_space=pltpu.VMEM),) * 2,
        scratch_shapes=[
            V((R, NX * DL), bf16),
            V((DL, VL), bf16),
            V((1, NX * DL), f32),
            V((16, R), jnp.int32),
            V((1, R), jnp.int32),
            V((1, R), f32),
            V(box, f32),
            V(tile, bf16),
            V((2, NY) + tile, bf16),
            V((NX, KT) + tile, bf16),
            V((VT,) + tile, f32),
            V((VT,) + tile, f32),
            V((VT,) + tile, f32),
            V((VT,) + tile, f32),
            V((2,) + tile, f32),
            V((2,) + tile, f32),
            V((VT,) + tile, f32),
            V((VT,) + tile, f32),
            V((VT,) + tile, jnp.int32),
            V((VT,) + tile, f32),
            V((VT,) + tile, f32),
            V((NY * NC, 2, 8, 128), f32),
            V((NZ, 2, 8, 128), f32),
            V((NY * NC, 8, 128), f32),
            V((NZ, 8, 128), f32),
            V((NX, VT) + tile, bf16),
            V((NX, VT) + tile, bf16),
            V((2 * NY, 128, VL), bf16),
            V((NX, 2, NY) + box, f32),
            V((NX, 2) + box, bf16),
            V((NX, 2) + box, bf16),
            V((NX, 2) + box, bf16),
            V((NX,) + box, bf16),
            V((NX,) + box, bf16),
            V((NX, 2) + box, bf16),
            V((NX, 2) + box, bf16),
            V((NX, 2) + box, bf16),
            V((NX, 2) + box, bf16),
            V((NZ,) + box, bf16),
            pltpu.SemaphoreType.DMA((6,)),
            pltpu.SemaphoreType.DMA((wires,)),
            pltpu.SemaphoreType.DMA((wires,)),
            pltpu.SemaphoreType.DMA((NX * 2,)),
            pltpu.SemaphoreType.DMA((NZ,)),
        ],
        compiler_params=pltpu.CompilerParams(
            collective_id=0, has_side_effects=True, vmem_limit_bytes=63 << 20
        ),
        name="head_grad",
    )(
        hidden,
        head,
        gain.reshape(1, -1),
        refusal_ids.T,
        refusal_count.reshape(1, -1),
        loss_scale.reshape(1, -1),
    )
    return grad, log_refusal.reshape(-1)


def solution(mesh):
    return jax.shard_map(
        shards,
        mesh=mesh,
        in_specs=(
            P("prompt", None),
            P("prompt", "vocab"),
            P(),
            P("prompt", None),
            P("prompt"),
            P("prompt"),
        ),
        out_specs=(P("prompt", "vocab"), P("prompt")),
        check_vma=False,
    )
```

```python
import functools

import jax
import jax.numpy as jnp
from jax import lax
from jax.experimental import pallas as pl
from jax.experimental.pallas import tpu as pltpu
from jax.sharding import PartitionSpec as P

epsilon = 1e-05
lowest = -1e30
f32 = jnp.float32
bf16 = jnp.bfloat16

NX, NY, NZ, NC = 4, 4, 8, 2
R = 128
DL = 2048
VL = 1024
T = 256
KT = DL // T
VT = VL // T


class Wires:
    def __init__(self, send, recv):
        self.send, self.recv, self.used, self.open = send, recv, 0, []

    def describe(self, src, dst, device, index):
        return pltpu.make_async_remote_copy(
            src_ref=src,
            dst_ref=dst,
            send_sem=self.send.at[index],
            recv_sem=self.recv.at[index],
            device_id=device,
            device_id_type=pl.DeviceIdType.MESH,
        )

    def start(self, src, dst, device):
        copy = self.describe(src, dst, device, self.used)
        self.used += 1
        copy.start()
        self.open.append(copy)
        return copy

    def close(self):
        for copy in self.open:
            copy.wait_send()


def kernel(
    hid_hbm, head_hbm, gain_hbm, ids_hbm, count_hbm, loss_hbm, grad_ref, log_ref,
    hid, head, gain_ref, ids_ref, count_ref, loss_ref, inv_v, nfar, nsend, nrm, ptwo, pright, pleft, pown, hl, hr, inl, inr,
    mask, eall, eref, st1, st2, rs1, rs2, gt, gs, lent, own32,
    ytwo, yright, yleft, yhl, yhr, yinl, yinr, fsend, xrecv, frecv,
    load_sems, send_sems, recv_sems, fsend_sems, frecv_sems,
):
    p = lax.axis_index("prompt")
    v = lax.axis_index("vocab")
    c = v % NC
    y = (v // NC) % NY
    z = v // (NC * NY)

    def at(x_=p, y_=y, z_=z, c_=c):
        return (x_, (z_ * NY + y_) * NC + c_)

    def x_by(d):
        return at(x_=(p + d) % NX)

    def y_by(d):
        return at(y_=(y + d) % NY)

    def z_by(d):
        return at(z_=(z + d) % NZ)

    j_own = y * NC + c

    def plane_by(d):
        j = (j_own + d) % (NY * NC)
        return at(y_=j // NC, c_=j % NC), j

    sibling = at(c_=1 - c)

    load_hid = pltpu.make_async_copy(hid_hbm, hid, load_sems.at[0])
    load_gain = pltpu.make_async_copy(gain_hbm, gain_ref, load_sems.at[1])
    load_head = pltpu.make_async_copy(head_hbm, head, load_sems.at[2])
    load_ids = pltpu.make_async_copy(ids_hbm, ids_ref, load_sems.at[3])
    load_count = pltpu.make_async_copy(count_hbm, count_ref, load_sems.at[4])
    load_loss = pltpu.make_async_copy(loss_hbm, loss_ref, load_sems.at[5])
    loads = (load_hid, load_gain, load_head, load_ids, load_count, load_loss)
    for load in loads:
        load.start()

    barrier = pltpu.get_barrier_semaphore()

    def greet(device):
        pl.semaphore_signal(
            barrier, inc=1, device_id=device, device_id_type=pl.DeviceIdType.MESH
        )

    for d in range(1, NX):
        greet(x_by(d))
    for d in range(1, NY * NC):
        greet(plane_by(d)[0])
    for d in range(1, NZ):
        greet(z_by(d))
    corners = [(1, 1), (1, NZ - 1), (NY - 1, 1), (NY - 1, NZ - 1)]

    def corner(i):
        return at(y_=(y + corners[i][0]) % NY, z_=(z + corners[i][1]) % NZ)

    for i in range(4):
        greet(corner(i))

    wires = Wires(send_sems, recv_sems)

    lane = lax.broadcasted_iota(jnp.int32, (R, 128), 1)
    sub = lax.broadcasted_iota(jnp.int32, (R, 128), 0)

    def columns_of(rows):
        return jnp.concatenate([rows, jnp.zeros((R - 8, 128), f32)], axis=0).T

    load_hid.wait()

    def square(j, acc):
        x = hid[:, pl.ds(pl.multiple_of(j * 1024, 1024), 1024)].astype(f32)
        x = x * x
        for i in range(8):
            acc = acc + x[:, i * 128 : (i + 1) * 128]
        return acc

    acc = lax.fori_loop(0, 8, square, jnp.zeros((R, 128), f32))
    inv = lax.rsqrt(jnp.sum(acc, axis=1, keepdims=True) / 8192.0 + epsilon)
    inv_v[...] = jnp.broadcast_to(inv, (R, 128))
    load_gain.wait()

    def normed(col):
        col = pl.multiple_of(col, T)
        x = hid[:, pl.ds(col, T)].astype(f32)
        return (x * inv * gain_ref[:, pl.ds(col, T)]).astype(bf16)

    def piece_of(cc, dy, dz):
        return cc * 4 + (y + dy) % 2 * 2 + (z + dz) % 2

    nfar[...] = normed((p + 2) % NX * DL + piece_of(c, 0, 0) * T)

    pl.semaphore_wait(barrier, (NX - 1) + (NY * NC - 1) + (NZ - 1) + 4)

    up, down = y_by(1), y_by(NY - 1)
    right, left = x_by(1), x_by(NX - 1)
    half, other_half = pl.ds(c * NY, NY), pl.ds((1 - c) * NY, NY)
    own_piece = piece_of(c, 0, 0)
    come2 = wires.start(nfar, nrm.at[2, own_piece], x_by(2))
    come, shared = {}, {}
    for i, d in ((0, 1), (1, NX - 1)):
        for k in range(NY):
            nsend[i, k] = normed((p + d) % NX * DL + (c * NY + k) * T)

    def rows_of(piece, i, n):
        return nrm.at[2, piece, pl.ds(i * (R // n), R // n)]

    sides = (up, down, z_by(1), z_by(NZ - 1))
    come2.wait_recv()
    spread_at = wires.used
    for i in range(4):
        part = rows_of(own_piece, i, 4)
        wires.start(part, part, corner(i))
    for i in range(4):
        part = rows_of(own_piece, i % 2, 2)
        wires.start(part, part, sides[i])

    come[3] = wires.start(nsend.at[0], nrm.at[3, half], right)
    come[1] = wires.start(nsend.at[1], nrm.at[1, half], left)

    def share_piece(dy, dz):
        whole = nrm.at[2, piece_of(c, dy, dz)]
        shared_at[dy, dz] = wires.used
        wires.start(whole, whole, sibling)

    shared_at = {}
    share_piece(0, 0)
    for k in range(KT):
        nrm[0, k] = normed(p * DL + k * T)
    for dy, dz, first in ((1, 0, 0), (0, 1, 2)):
        for i in range(2):
            part = rows_of(piece_of(c, dy, dz), i, 2)
            wires.describe(part, part, sides[first + i], spread_at + 4 + first + i).wait_recv()
        share_piece(dy, dz)
    for i in range(4):
        part = rows_of(piece_of(c, 1, 1), i, 4)
        wires.describe(part, part, corner(i), spread_at + i).wait_recv()
    share_piece(1, 1)

    def share(slot):
        come[slot].wait_recv()
        rows = nrm.at[slot, half]
        shared[slot, "at"] = wires.used
        wires.start(rows, rows, sibling)

    def wait_share(slot):
        if slot == 2:
            for (dy, dz), index in shared_at.items():
                rows = nrm.at[2, piece_of(1 - c, dy, dz)]
                wires.describe(rows, rows, sibling, index).wait_recv()
        else:
            rows = nrm.at[slot, other_half]
            wires.describe(rows, rows, sibling, shared[slot, "at"]).wait_recv()

    def partial(s, t):
        lhs = jnp.concatenate([nrm[s, k] for k in range(KT)], axis=1)
        return jnp.dot(lhs, head[:, t * T : (t + 1) * T], preferred_element_type=f32)

    load_head.wait()
    wait_share(2)
    ch_l, ch_r, cin_l, cin_r = {}, {}, {}, {}
    for t in (0, 2, 1, 3):
        ptwo[t] = partial(2, t)
        if t < 2:
            ch_l[t] = wires.start(ptwo.at[t], hl.at[t], right)
        else:
            ch_r[t - 2] = wires.start(ptwo.at[t], hr.at[t - 2], left)
    share(3)
    share(1)
    wait_share(1)
    for t in (2, 3):
        pright[t] = partial(1, t)
        cin_l[t] = wires.start(pright.at[t], inl.at[t], right)
    wait_share(3)
    for t in (0, 1):
        pleft[t] = partial(3, t)
        cin_r[t] = wires.start(pleft.at[t], inr.at[t], left)
    for t in (0, 1):
        pright[t] = partial(1, t)
        pleft[t + 2] = partial(3, t + 2)
    for t in (0, 1):
        ch_l[t].wait_recv()
        pright[t] = pright[t] + hl[t]
        cin_l[t] = wires.start(pright.at[t], inl.at[t], right)
        ch_r[t].wait_recv()
        pleft[t + 2] = pleft[t + 2] + hr[t]
        cin_r[t + 2] = wires.start(pleft.at[t + 2], inr.at[t + 2], left)
    lend = {}
    for b in range(2 * NY):
        rows = pl.ds(pl.multiple_of((b * NC + 1 - c) * 128, 128), 128)
        lend[b] = wires.start(head.at[rows], lent.at[b], sibling)
    for t in range(VT):
        pown[t] = partial(0, t)

    load_ids.wait()
    load_count.wait()
    load_loss.wait()
    ids = jnp.concatenate([ids_ref[...], jnp.zeros((R - 16, 128), jnp.int32)], axis=0).T
    cl = jnp.where(
        sub == 0,
        jnp.broadcast_to(count_ref[...].astype(f32), (R, 128)),
        jnp.where(sub == 1, jnp.broadcast_to(loss_ref[...], (R, 128)), 0.0),
    ).T
    count_col, loss_col = cl[:, 0:1], cl[:, 1:2]
    wide = lax.broadcasted_iota(jnp.int32, (R, T), 1)
    for t in range(VT):
        hit = jnp.zeros((R, T), jnp.int32)
        for k in range(16):
            here = ids[:, k : k + 1] - (v * VL + t * T)
            here = jnp.where(count_col > float(k), here, -1)
            hit = jnp.where(wide == here, 1, hit)
        mask[t] = hit

    m_all = jnp.full((R, T), -3e38, f32)
    m_ref = jnp.full((R, T), lowest, f32)
    for t in (2, 3, 0, 1):
        cin_l[t].wait_recv()
        cin_r[t].wait_recv()
        logit = pown[t] + inl[t] + inr[t]
        pown[t] = logit
        m_all = jnp.maximum(m_all, logit)
        m_ref = jnp.maximum(m_ref, jnp.where(mask[t] > 0, logit, lowest))
    m_all = jnp.max(m_all, axis=1, keepdims=True)
    m_ref = jnp.max(m_ref, axis=1, keepdims=True)
    s_all = jnp.zeros((R, T), f32)
    s_ref = jnp.zeros((R, T), f32)
    for t in range(VT):
        logit = pown[t]
        e = jnp.exp(logit - m_all)
        r = jnp.exp(jnp.where(mask[t] > 0, logit - m_ref, lowest))
        eall[t] = e
        eref[t] = r
        s_all = s_all + e
        s_ref = s_ref + r
    s_all = jnp.sum(s_all, axis=1, keepdims=True)
    s_ref = jnp.sum(s_ref, axis=1, keepdims=True)

    packed = jnp.where(lane == 0, m_all, jnp.zeros((R, 128), f32))
    packed = jnp.where(lane == 1, m_ref, packed)
    packed = jnp.where(lane == 8, s_all, packed)
    packed = jnp.where(lane == 9, s_ref, packed)
    packed = packed.T
    st1[j_own, 0] = packed[0:8]
    st1[j_own, 1] = packed[8:16]

    far_first = (4, 3, 5, 2, 6, 1, 7)

    def spread_plane(buf):
        first = wires.used
        for d in far_first:
            wires.start(buf.at[j_own], buf.at[j_own], plane_by(d)[0])
        return first

    def await_plane(buf, first):
        for i, d in enumerate(far_first):
            device, j = plane_by(NY * NC - d)
            wires.describe(buf.at[j], buf.at[j], device, first + i).wait_recv()

    def spread_line(buf):
        first = wires.used
        for d in far_first:
            wires.start(buf.at[z], buf.at[z], z_by(d))
        return first

    def await_line(buf, first):
        for i, d in enumerate(far_first):
            zz = (z + NZ - d) % NZ
            wires.describe(buf.at[zz], buf.at[zz], at(z_=zz), first + i).wait_recv()

    def merged(buf, n):
        peak = buf[0, 0]
        for j in range(1, n):
            peak = jnp.maximum(peak, buf[j, 0])
        total = buf[0, 1] * jnp.exp(buf[0, 0] - peak)
        for j in range(1, n):
            total = total + buf[j, 1] * jnp.exp(buf[j, 0] - peak)
        return peak, total

    first = spread_plane(st1)
    await_plane(st1, first)
    peak, total = merged(st1, NY * NC)
    st2[z, 0] = peak
    st2[z, 1] = total
    first = spread_line(st2)
    await_line(st2, first)
    peak, total = merged(st2, NZ)
    row8 = lax.broadcasted_iota(jnp.int32, (8, 128), 0)
    lse = peak + jnp.log(jnp.where(row8 < 2, total, 1.0))
    log_ref[...] = lse[1:2] - lse[0:1]
    lse_cols = columns_of(lse)
    f_all = loss_col * jnp.exp(m_all - lse_cols[:, 0:1])
    f_ref = loss_col * jnp.exp(m_ref - lse_cols[:, 1:2])

    rt = jnp.zeros((R, T), f32)
    to_right, to_left = {}, {}
    def gather(t_r, t_l):
        to_right[t_r] = wires.start(gt.at[0, t_r], gt.at[3, t_r], right)
        to_left[t_l] = wires.start(gt.at[0, t_l], gt.at[1, t_l], left)

    for pair in ((0, 2), (1, 3)):
        for t in pair:
            g = eref[t] * f_ref - eall[t] * f_all
            g = g.astype(bf16)
            gt[0, t] = g
            rt = rt + g.astype(f32) * pown[t]
        gather(*pair)
    gather(2, 0)
    gather(3, 1)
    lot = {}

    def to_sibling(s, t):
        lot[s, t] = wires.start(gt.at[s, t], gs.at[s, t], sibling)

    for t in (0, 2, 1, 3):
        to_sibling(0, t)
    rt = jnp.sum(rt, axis=1, keepdims=True)
    rs1[j_own] = jnp.where(lane == 0, rt, jnp.zeros((R, 128), f32)).T[0:8]
    rt_first = spread_plane(rs1)

    yl2, yr2, yl, yr = {}, {}, {}, {}
    y1, y2, y3 = ((y + d) % NY for d in (1, 2, 3))

    def multiply(s):
        def times(block, tiles):
            rhs = jnp.concatenate([tiles[s, t] for t in range(VT)], axis=1).T
            return jnp.dot(block, rhs, preferred_element_type=f32).reshape(NY, 128, R)

        for zl in range(2):
            rows = [
                pl.multiple_of(((zl * NY + yy) * NC + c) * 128, 128)
                for yy in range(NY)
            ]
            here = jnp.concatenate([head[pl.ds(row, 128), :] for row in rows], axis=0)
            own32[s, zl] = times(here, gt)
        for t in range(VT):
            lot[s, t].wait_recv()
        for zl in range(2):
            block = lent[zl * NY : (zl + 1) * NY].reshape(NY * 128, VL)
            own32[s, zl] = own32[s, zl] + times(block, gs)
            y_first(s, zl)

    def y_first(s, zl):
        ytwo[s, zl] = own32[s, zl, y2].astype(bf16)
        if zl == 0:
            yl2[s] = wires.start(ytwo.at[s, 0], yhl.at[s], up)
            yleft[s, 0] = own32[s, 0, y3].astype(bf16)
            yr[s, 0] = wires.start(yleft.at[s, 0], yinr.at[s, 0], down)
        else:
            yr2[s] = wires.start(ytwo.at[s, 1], yhr.at[s], down)
            yright[s, 1] = own32[s, 1, y1].astype(bf16)
            yl[s, 1] = wires.start(yright.at[s, 1], yinl.at[s, 1], up)

    def y_second(s):
        yl2[s].wait_recv()
        yright[s, 0] = (own32[s, 0, y1] + yhl[s].astype(f32)).astype(bf16)
        yl[s, 0] = wires.start(yright.at[s, 0], yinl.at[s, 0], up)
        yr2[s].wait_recv()
        yleft[s, 1] = (own32[s, 1, y3] + yhr[s].astype(f32)).astype(bf16)
        yr[s, 1] = wires.start(yleft.at[s, 1], yinr.at[s, 1], down)

    def place(s, zl):
        return pltpu.make_async_remote_copy(
            src_ref=xrecv.at[s, zl],
            dst_ref=frecv.at[z],
            send_sem=fsend_sems.at[s * 2 + zl],
            recv_sem=frecv_sems.at[z],
            device_id=at(z_=(p + NX - s) % NX * 2 + zl),
            device_id_type=pl.DeviceIdType.MESH,
        )

    move = {}

    def y_third(s):
        for zl in (1, 0):
            yl[s, zl].wait_recv()
            yr[s, zl].wait_recv()
            out = own32[s, zl, y]
            out = out + yinl[s, zl].astype(f32) + yinr[s, zl].astype(f32)
            if s:
                fsend[s, zl] = out.astype(bf16)
                move[s, zl] = wires.start(fsend.at[s, zl], xrecv.at[s, zl], x_by(s))
            else:
                xrecv[s, zl] = out.astype(bf16)

    def z_out(s):
        for zl in (1, 0):
            if s:
                move[s, zl].wait_recv()
            there_z = (p + NX - s) % NX * 2 + zl

            @pl.when(z != there_z)
            def _():
                place(s, zl).start()

            @pl.when(z == there_z)
            def _():
                frecv[z] = xrecv[s, zl]

    for b in range(2 * NY):
        lend[b].wait_recv()
    multiply(0)
    for t in (0, 1):
        to_right[t].wait_recv()
        wires.start(gt.at[3, t], gt.at[2, t], right)
        to_left[t + 2].wait_recv()
        wires.start(gt.at[1, t + 2], gt.at[2, t + 2], left)
        to_sibling(3, t)
        to_sibling(1, t + 2)
    forward = wires.used - 8
    for t in (2, 3):
        to_right[t].wait_recv()
        to_sibling(3, t)
        to_left[t - 2].wait_recv()
        to_sibling(1, t - 2)
    y_second(0)
    multiply(3)
    multiply(1)
    y_third(0)
    z_out(0)
    await_plane(rs1, rt_first)
    total = rs1[0]
    for j in range(1, NY * NC):
        total = total + rs1[j]
    rs2[z] = total
    rt_first = spread_line(rs2)
    for t in (0, 1):
        for i, tile, device in ((0, t, left), (1, t + 2, right)):
            wires.describe(
                gt.at[2, tile], gt.at[2, tile], device, forward + 4 * t + i
            ).wait_recv()
            to_sibling(2, tile)
    multiply(2)
    y_second(3)
    y_second(1)
    y_second(2)
    y_third(2)
    y_third(3)
    y_third(1)
    z_out(3)
    z_out(1)
    await_line(rs2, rt_first)
    total = rs2[0]
    for j in range(1, NZ):
        total = total + rs2[j]
    rt_col = columns_of(total)[:, 0:1]
    z_out(2)

    own_cols = pl.ds(pl.multiple_of(v * 128, 128), 128)
    inv = inv_v[...]
    minus = hid[:, own_cols].astype(f32) * (inv * inv / 8192.0) * rt_col
    scale = inv * gain_ref[:, own_cols]
    for zs in range(NZ):

        @pl.when(zs != z)
        def _():
            pltpu.make_async_remote_copy(
                src_ref=frecv.at[zs],
                dst_ref=frecv.at[zs],
                send_sem=fsend_sems.at[0],
                recv_sem=frecv_sems.at[zs],
                device_id=at(z_=zs),
                device_id_type=pl.DeviceIdType.MESH,
            ).wait_recv()

    total = frecv[0].astype(f32)
    for zs in range(1, NZ):
        total = total + frecv[zs].astype(f32)
    grad_ref[...] = scale * total.T - minus

    wires.close()
    for s in range(NX):
        for zl in range(2):

            @pl.when(z != (p + NX - s) % NX * 2 + zl)
            def _():
                place(s, zl).wait_send()


def shards(hidden, head, gain, refusal_ids, refusal_count, loss_scale):
    V = pltpu.VMEM
    tile = (R, T)
    box = (R, 128)
    wires = 140
    grad, log_refusal = pl.pallas_call(
        kernel,
        out_shape=(
            jax.ShapeDtypeStruct((R, 128), f32),
            jax.ShapeDtypeStruct((1, R), f32),
        ),
        in_specs=[pl.BlockSpec(memory_space=pltpu.HBM)] * 6,
        out_specs=(pl.BlockSpec(memory_space=pltpu.VMEM),) * 2,
        scratch_shapes=[
            V((R, NX * DL), bf16),
            V((DL, VL), bf16),
            V((1, NX * DL), f32),
            V((16, R), jnp.int32),
            V((1, R), jnp.int32),
            V((1, R), f32),
            V(box, f32),
            V(tile, bf16),
            V((2, NY) + tile, bf16),
            V((NX, KT) + tile, bf16),
            V((VT,) + tile, f32),
            V((VT,) + tile, f32),
            V((VT,) + tile, f32),
            V((VT,) + tile, f32),
            V((2,) + tile, f32),
            V((2,) + tile, f32),
            V((VT,) + tile, f32),
            V((VT,) + tile, f32),
            V((VT,) + tile, jnp.int32),
            V((VT,) + tile, f32),
            V((VT,) + tile, f32),
            V((NY * NC, 2, 8, 128), f32),
            V((NZ, 2, 8, 128), f32),
            V((NY * NC, 8, 128), f32),
            V((NZ, 8, 128), f32),
            V((NX, VT) + tile, bf16),
            V((NX, VT) + tile, bf16),
            V((2 * NY, 128, VL), bf16),
            V((NX, 2, NY) + box, f32),
            V((NX, 2) + box, bf16),
            V((NX, 2) + box, bf16),
            V((NX, 2) + box, bf16),
            V((NX,) + box, bf16),
            V((NX,) + box, bf16),
            V((NX, 2) + box, bf16),
            V((NX, 2) + box, bf16),
            V((NX, 2) + box, bf16),
            V((NX, 2) + box, bf16),
            V((NZ,) + box, bf16),
            pltpu.SemaphoreType.DMA((6,)),
            pltpu.SemaphoreType.DMA((wires,)),
            pltpu.SemaphoreType.DMA((wires,)),
            pltpu.SemaphoreType.DMA((NX * 2,)),
            pltpu.SemaphoreType.DMA((NZ,)),
        ],
        compiler_params=pltpu.CompilerParams(
            collective_id=0, has_side_effects=True, vmem_limit_bytes=63 << 20
        ),
        name="head_grad",
    )(
        hidden,
        head,
        gain.reshape(1, -1),
        refusal_ids.T,
        refusal_count.reshape(1, -1),
        loss_scale.reshape(1, -1),
    )
    return grad, log_refusal.reshape(-1)


def solution(mesh):
    return jax.shard_map(
        shards,
        mesh=mesh,
        in_specs=(
            P("prompt", None),
            P("prompt", "vocab"),
            P(),
            P("prompt", None),
            P("prompt"),
            P("prompt"),
        ),
        out_specs=(P("prompt", "vocab"), P("prompt")),
        check_vma=False,
    )
```
